256 devices in a mesh: stream: 16 (over y, x), span: 16 (over z, core).
Axes of the slice: x: 4, y: 4, z: 8, core: 2. Of those that a mesh axis runs over, the one named last changes fastest.
Arguments:
- forcing: float32 [5, 512, 512, 128], P(None, 'span', 'stream'), may hold values from -6 to 6
- initial_state: float32 [256, 5, 2, 512, 128], P('span', None, None, 'stream'), may hold values from -4 to 4
- diagonal: float32 [5, 512, 128], replicated, may hold values from 1.5 to 4
- span_speed: float32 [5], replicated, may hold values from 0.3 to 3
- coupling: float32 [4, 5, 5], replicated, may hold values from -1.25 to 1.25
- stiffener_mask: int32 [512, 128], replicated, may hold values 0 or 1
- face_index: int32 [2, 32768], P(None, ('stream', 'span')), may hold values from 0 to 1023
- mode_shapes: float32 [2, 2, 32768], P(None, None, ('stream', 'span')), may hold values from -12 to 12
Outputs:
- flow: float32 [256, 5, 2, 512, 128], P('span', None, None, 'stream')
- forces: float32 [2, 2], replicated
The draws below stay inside these ranges and needn't reach their ends.
All inputs are finite; a program needn't handle non-finite values.
Results may differ from the reference program's by a relative error of at most 0.00025.
Values sent between devices are 32-bit elements; how exact they have to be, the bound alone decides.
A program may use at most 192 MiB of HBM per device.

```python
import math
import jax
import jax.numpy as jnp
from jax import lax

C = 5
M = 2
NY = 128
XD = 32
ZD = 32
FACE_DEV = 128
NX = 512
NZ = 512
KW = 256
FACES = 32768
N_SPAN = 16


def draw_mode_shapes(key, part):
    ramp = 1.0 + 2.0 * jnp.arange(FACES, dtype=jnp.float32) / FACES
    base = jnp.clip(jax.random.normal(key, (M, 2, FACES), jnp.float32), -4.0, 4.0)
    return base * ramp


def place_ends(drawn, own_key, smallest, top_value):
    longest = drawn.shape.index(max(drawn.shape))
    spots = []
    for shift in (0, 1):
        where = [jax.random.randint(jax.random.fold_in(own_key, axis), (), 0, length) for axis, length in enumerate(drawn.shape)]
        where[longest] = (where[longest] + shift) % drawn.shape[longest]
        spots.append(tuple(where))
    return drawn.at[spots[0]].set(smallest).at[spots[1]].set(top_value)


def block_levels(rng, shape, split, least, high):
    def one(axis_at, parts):
        heights = jax.random.uniform(jax.random.fold_in(jax.random.fold_in(rng, 6), axis_at), (parts,), jnp.float32, least / len(split), high / len(split))
        return jnp.repeat(jnp.exp(heights), shape[axis_at] // parts).reshape((-1,) + (1,) * (len(shape) - axis_at - 1))

    loudness = one(*split[0])
    for cut in split[1:]:
        loudness = loudness * one(*cut)
    return loudness


def noise(own_key, dims, deviation, limit, pieces=(), held_as=jnp.bfloat16):
    array = jax.random.normal(own_key, dims, jnp.float32) * deviation
    if len(pieces) > 0:
        array = block_levels(own_key, dims, pieces, -0.22, 0.18) * array
    return jnp.clip(array, min=-limit, max=limit).astype(held_as)


def setup_inputs(seed: int = 0) -> dict:
    splits = jax.random.split(jax.random.key(seed), 9)
    return {
        "forcing": noise(splits[0], (C, NZ, NX, NY), 1.0, 6.0, ((1, 16), (2, 16)), jnp.float32),
        "initial_state": noise(splits[1], (KW, C, 2, NX, NY), 0.5, 4.0, ((0, 16), (3, 16)), jnp.float32),
        "diagonal": jnp.clip(jax.random.uniform(splits[2], (C, NX, NY), jnp.float32, 1.5, 4.0), 1.5, 4.0),
        "span_speed": jnp.clip(jnp.exp(jax.random.uniform(splits[3], (C,), jnp.float32, math.log(0.3), math.log(3.0))), 0.3, 3.0),
        "coupling": noise(splits[4], (4, C, C), (4 * C) ** -0.5, 1.25, (), jnp.float32),
        "stiffener_mask": place_ends((jax.random.randint(splits[5], (NX, NY), 0, 8) < 1).astype(jnp.int32), jax.random.fold_in(splits[5], 1), 0, 1),
        "face_index": place_ends(jax.random.randint(splits[6], (M, FACES), 0, XD * ZD), jax.random.fold_in(splits[6], 1), 0, (XD * ZD) - 1).astype(jnp.int32),
        "mode_shapes": draw_mode_shapes(jax.random.fold_in(splits[8], 71), 0),
    }


def wave_table(z_index, k_index, span_total):
    phase_index = z_index[:, None] * k_index[None, :] % span_total
    phase = phase_index.astype(jnp.float32) * (2.0 * math.pi / span_total)
    norm_factor = 1.0 / math.sqrt(span_total)
    return jnp.stack([jnp.cos(phase), -jnp.sin(phase)], axis=-1) * norm_factor

def inverse_table(k_index, z_index, span_total):
    tab = wave_table(z_index, k_index, span_total)
    fold_weight = jnp.where(k_index == 0, 1.0, 2.0).astype(jnp.float32)
    return jnp.transpose(tab, (1, 2, 0)) * fold_weight[:, None, None]

def relax_sweep(state_ext, rhs, diag_part, keep, wavenumber, span_speed, coupling):
    hi = lax.Precision.HIGHEST
    padded = jnp.pad(state_ext, ((0, 0), (0, 0), (0, 0), (0, 0), (1, 1)))
    neighbours = jnp.einsum('cd,kdrxy->kcrxy', coupling[0], padded[:, :, :, 2:, 1:-1], precision=hi)
    neighbours = neighbours + jnp.einsum('cd,kdrxy->kcrxy', coupling[1], padded[:, :, :, :-2, 1:-1], precision=hi)
    neighbours = neighbours + jnp.einsum('cd,kdrxy->kcrxy', coupling[2], padded[:, :, :, 1:-1, 2:], precision=hi)
    neighbours = neighbours + jnp.einsum('cd,kdrxy->kcrxy', coupling[3], padded[:, :, :, 1:-1, :-2], precision=hi)
    defect = rhs - neighbours
    span_part = wavenumber[:, None, None, None] * span_speed[None, :, None, None]
    diag_b = diag_part[None]
    modulus = diag_b * diag_b + span_part * span_part
    real_part = (diag_b * defect[:, :, 0] + span_part * defect[:, :, 1]) / modulus
    imag_part = (diag_b * defect[:, :, 1] - span_part * defect[:, :, 0]) / modulus
    return jnp.stack([real_part, imag_part], axis=2) * keep

def pad_stream(state):
    return jnp.pad(state, ((0, 0), (0, 0), (0, 0), (1, 1), (0, 0)))

def reference(forcing, initial_state, diagonal, span_speed, coupling, stiffener_mask, face_index, mode_shapes):
    hi = lax.Precision.HIGHEST
    z_all = jnp.arange(NZ, dtype=jnp.int32)
    k_all = jnp.arange(KW, dtype=jnp.int32)
    dft_table = wave_table(z_all, k_all, NZ)
    rhs = jnp.einsum('czxy,zkr->kcrxy', forcing, dft_table, precision=hi)
    wavenumber = k_all.astype(jnp.float32) * (2.0 * math.pi / NZ)
    keep = (1 - stiffener_mask).astype(jnp.float32)

    def solve_wave(inputs):
        rhs_one, start_one, wave_one = inputs
        first_pass = relax_sweep(pad_stream(start_one), rhs_one, diagonal, keep, wave_one, span_speed, coupling)
        return relax_sweep(pad_stream(first_pass), rhs_one, diagonal, keep, wave_one, span_speed, coupling)
    flow = lax.map(solve_wave, (rhs[:, None], initial_state[:, None], wavenumber[:, None]))[:, 0]
    wall = flow[:, C - 1, :, :, 0]
    pressure = jnp.einsum('krx,krz->zx', wall, inverse_table(k_all, z_all, NZ), precision=hi)
    face_all = jnp.arange(FACES, dtype=jnp.int32)
    device_of = face_all // FACE_DEV
    stream_of = device_of // N_SPAN
    span_of = device_of % N_SPAN
    z_cell = span_of[None, :] * ZD + face_index // XD
    x_cell = stream_of[None, :] * XD + face_index % XD
    face_values = pressure[z_cell, x_cell]
    forces = lax.optimization_barrier(jnp.sum(face_values[:, None, :] * mode_shapes, axis=-1)) / math.sqrt(FACES)
    return (flow, forces)
```

```python
import functools
import math

import jax
import jax.numpy as jnp
import numpy as np
from jax import lax
from jax.experimental import pallas as pl
from jax.experimental.pallas import tpu as pltpu
from jax.sharding import PartitionSpec as P

MESH = pl.DeviceIdType.MESH
S = 16
N = 16
K = 16
C = 5
X = 32
Z = 32
Y = 128
NZ = 512
KR = 2 * K
CHUNKS = X * C // S
f32 = jnp.float32
bf16 = jnp.bfloat16


def table_rows():
    z = np.arange(NZ)
    k = np.arange(NZ // 2)
    phase = (k[:, None] * z[None, :] % NZ) * (2.0 * math.pi / NZ)
    both = np.stack([np.cos(phase), -np.sin(phase)], 0) / math.sqrt(NZ)
    rows = both.reshape(2, S, K, NZ).transpose(1, 0, 2, 3).reshape(NZ, NZ)
    exact = rows.astype(np.float32)
    high = exact.astype(jnp.bfloat16)
    low = (exact - high.astype(np.float32)).astype(jnp.bfloat16)
    return high, low


def split(v):
    high = v.astype(bf16)
    return high, (v - high.astype(f32)).astype(bf16)


def dot3(ah, al, bh, bl):
    d = functools.partial(jnp.dot, preferred_element_type=f32)
    return d(ah, bh) + (d(ah, bl) + d(al, bh))


def cell(order):
    half = lax.div(order, 2)
    return jnp.where(lax.rem(order, 2) == 0, half, X - 1 - half)


def row_of(j, p):
    rho = j * S + p
    return cell(lax.div(rho, C)), lax.rem(rho, C)


def done_after(j):
    return lax.div((j + 1) * S, C)


def loop(lo, hi, body):
    def step(i, carry):
        body(i)
        return carry

    lax.fori_loop(lo, hi, step, 0)


def kernel(
    forcing, init, diag, speed, coup, mask, faces, modes, thigh, tlow,
    flow, forces,
    th, tl, fbuf, sbuf, rhs, q0, q1, q2, near0, alpha, beta, coef, dv, kv, bv,
    fv, mv, wallm, gv, wall, sum1, sum2, fown, mown,
    sem_t, sem_q, sem_d, sem_f, send1, recv1, send2, recv2,
    hs0, hr0, hs1, hr1, fs, fr, ps, pr, osem,
):
    me = lax.axis_index("span")
    st = lax.axis_index("stream")
    first, last = st == 0, st == N - 1
    inner_l, inner_r = st > 0, st < N - 1

    def remote(src, dst, ss, rs, axis, to):
        return pltpu.make_async_remote_copy(
            src_ref=src, dst_ref=dst, send_sem=ss, recv_sem=rs, device_id={axis: to}, device_id_type=MESH
        )

    def arrived(ref, sem):
        pltpu.make_async_copy(ref, ref, sem).wait()

    barrier = pltpu.get_barrier_semaphore()

    def greet(i):
        pl.semaphore_signal(barrier, inc=1, device_id={"span": lax.rem(me + i, S)}, device_id_type=MESH)
        pl.semaphore_signal(barrier, inc=1, device_id={"stream": lax.rem(st + i, N)}, device_id_type=MESH)

    loop(1, S, greet)

    x0 = pl.multiple_of(st * X, X)
    cp_d = pltpu.make_async_copy(diag.at[:, pl.ds(x0, X), :], dv, sem_d.at[0])
    cp_k = pltpu.make_async_copy(mask.at[pl.ds(x0, X), :], kv, sem_d.at[1])
    cp_d.start()
    cp_k.start()
    cp_h = pltpu.make_async_copy(thigh, th, sem_t.at[0])
    cp_l = pltpu.make_async_copy(tlow, tl, sem_t.at[1])
    cp_h.start()
    cp_l.start()
    cp_f = pltpu.make_async_copy(faces, fown, sem_f.at[0])
    cp_m = pltpu.make_async_copy(modes, mown, sem_f.at[1])
    cp_f.start()
    cp_m.start()

    mine = pl.multiple_of(me * Z, Z)

    def own_rows(j):
        x, c = row_of(j, me)
        pltpu.make_async_copy(forcing.at[c, :, x, 0, :], fbuf.at[j, pl.ds(mine, Z), :], recv1.at[j]).start()

    loop(0, CHUNKS, own_rows)

    def load_state(x):
        for c in range(C):
            for r in range(2):
                pltpu.make_async_copy(
                    init.at[:, c, r, x, 0, :], q0.at[x + 1, c, pl.ds(r * K, K), :], sem_q
                ).start()

    loop(0, X, load_state)

    for a in range(4):
        for c in range(C):
            for d in range(C):
                coef[a * 25 + c * 5 + d] = jnp.full((8, Y), coup[a, c, d], f32)
    k_index = (me * K + lax.broadcasted_iota(jnp.int32, (K, Y), 0)).astype(f32)
    for c in range(C):
        bv[c] = k_index * (2.0 * math.pi / NZ) * speed[c]

    @pl.when(first)
    def _():
        q0[0] = jnp.zeros((C, KR, Y), f32)
        q1[0] = jnp.zeros((C, KR, Y), f32)

    @pl.when(last)
    def _():
        q0[X + 1] = jnp.zeros((C, KR, Y), f32)
        q1[X + 1] = jnp.zeros((C, KR, Y), f32)

    cp_f.wait()
    cp_m.wait()
    fv[me] = fown[...]
    mv[me] = mown[...]
    pl.semaphore_wait(barrier, 2 * S - 2)

    def halo0(c):
        for r in range(2):
            rows = pl.ds(r * K, K)

            @pl.when(inner_l)
            def _():
                remote(init.at[:, c, r, 0, 0, :], q0.at[X + 1, c, rows, :], hs0.at[0], hr0.at[1], "stream", st - 1).start()

            @pl.when(inner_r)
            def _():
                remote(init.at[:, c, r, X - 1, 0, :], q0.at[0, c, rows, :], hs0.at[1], hr0.at[0], "stream", st + 1).start()

    loop(0, C, halo0)

    def send_forcing(j):
        def one(i):
            t = lax.rem(me + i, S)
            x, c = row_of(j, t)
            remote(
                forcing.at[c, :, x, 0, :], fbuf.at[j, pl.ds(mine, Z), :], send1, recv1.at[j], "span", t
            ).start()

        loop(1, S, one)

    def send_faces(i):
        t = lax.rem(me + i, S)
        remote(fown, fv.at[me], fs.at[0], fr.at[0], "span", t).start()
        remote(mown, mv.at[me], fs.at[1], fr.at[1], "span", t).start()

    send_forcing(0)
    loop(1, S, send_faces)
    loop(1, CHUNKS, send_forcing)

    cp_d.wait()
    cp_k.wait()

    def factors(x):
        keep = 1.0 - kv[pl.ds(x, 1), :].astype(f32)
        for c in range(C):
            a = jnp.broadcast_to(dv[c, pl.ds(x, 1), :], (K, Y))
            b = bv[c]
            scale = keep / (a * a + b * b)
            alpha[x, c] = a * scale
            beta[x, c] = b * scale

    loop(0, X, factors)

    lane = lax.broadcasted_iota(jnp.int32, (KR, Y), 1)

    def near(q, x):
        acc = [None] * C
        for d in range(C):
            here = q[x + 1, d]
            up = jnp.where(lane < Y - 1, pltpu.roll(here, Y - 1, 1), 0.0)
            down = jnp.where(lane > 0, pltpu.roll(here, 1, 1), 0.0)
            for a, v in enumerate((q[x + 2, d], q[x, d], up, down)):
                v = v.reshape(4, 8, Y)
                for c in range(C):
                    term = coef[a * 25 + c * 5 + d][None] * v
                    acc[c] = term if acc[c] is None else acc[c] + term
        return [v.reshape(KR, Y) for v in acc]

    arrived(q0.at[pl.ds(1, X)], sem_q)

    @pl.when(inner_l)
    def _():
        arrived(q0.at[0], hr0.at[0])

    @pl.when(inner_r)
    def _():
        arrived(q0.at[X + 1], hr0.at[1])

    def first_near(x):
        for c, v in enumerate(near(q0, x)):
            near0[x, c] = v

    loop(0, X, first_near)

    cp_h.wait()
    cp_l.wait()

    def transform(j):
        arrived(fbuf.at[j], recv1.at[j])
        fh, fl = split(fbuf[j])

        def rows(i):
            part = pl.ds(pl.multiple_of(i * 128, 128), 128)
            sbuf[j, part, :] = dot3(th[part, :], tl[part, :], fh, fl)

        for i in range(4):
            rows(i)
        x, c = row_of(j, me)
        rhs[x, c] = sbuf[j, pl.ds(mine, KR), :]

        def one(i):
            t = lax.rem(me + i, S)
            rows_t = pl.ds(pl.multiple_of(t * KR, KR), KR)
            remote(sbuf.at[j, rows_t, :], rhs.at[x, c], send2, recv2.at[j], "span", t).start()

        loop(1, S, one)

    loop(0, CHUNKS, transform)

    arrived(fv.at[pl.ds(0, S - 1)], fr.at[0])
    arrived(mv.at[pl.ds(0, S - 1)], fr.at[1])
    z_row = lax.broadcasted_iota(jnp.int32, (Z, 128), 0)
    x_row = lax.broadcasted_iota(jnp.int32, (128, 128), 0)

    def scatter(s):
        total = jnp.zeros((Z, 128), f32)
        for m in range(2):
            index = fv[s, pl.ds(m, 1), :]
            at_z = z_row == lax.div(index, X)
            for r in range(2):
                placed = (x_row == lax.rem(index, X) + (2 * m + r) * X).astype(f32)
                value = jnp.where(at_z, mv[s, m, pl.ds(r, 1), :], 0.0)
                total = total + lax.dot_general(
                    value, placed, (((1,), (1,)), ((), ())),
                    precision=lax.Precision.HIGHEST, preferred_element_type=f32,
                )
        wallm[pl.ds(pl.multiple_of(s * Z, Z), Z), :] = total

    loop(0, S, scatter)
    wh, wl = split(wallm[...])
    own_k = pl.ds(pl.multiple_of(me * KR, KR), KR)
    row = lax.broadcasted_iota(jnp.int32, (KR, Y), 0)
    zero_k = jnp.logical_and(me == 0, lax.rem(row, K) == 0)
    weight = jnp.where(zero_k, 1.0, 2.0)
    gv[...] = weight * dot3(th[own_k, :], tl[own_k, :], wh, wl)
    wall[...] = jnp.zeros((KR, 128), f32)

    def invert(x, c, d):
        re, im = d[:K], d[K:]
        al, be = alpha[x, c], beta[x, c]
        return al * re + be * im, al * im - be * re

    def sweep1(order):
        x = cell(order)
        for c in range(C):
            re, im = invert(x, c, rhs[x, c] - near0[x, c])
            q1[x + 1, c, 0:K] = re
            q1[x + 1, c, K:KR] = im

    def sweep2(order):
        x = cell(order)
        for c, v in enumerate(near(q1, x)):
            re, im = invert(x, c, rhs[x, c] - v)
            q2[x, c, 0:K] = re
            q2[x, c, K:KR] = im
            if c == C - 1:
                at = jnp.concatenate([re, im], 0)[:, 0:1]
                wall[...] += jnp.where(lax.rem(lane, X) == x, at, 0.0)
        for c in range(C):
            for r in range(2):
                pltpu.make_async_copy(
                    q2.at[x, c, pl.ds(r * K, K), :], flow.at[:, c, r, x, 0, :], osem
                ).start()

    def wait_chunk(j):
        pltpu.make_async_copy(rhs.at[pl.ds(0, 3)], rhs.at[pl.ds(0, 3)], recv2.at[j]).wait()

    wait_chunk(0)
    loop(0, S // C, sweep1)

    @pl.when(inner_l)
    def _():
        remote(q1.at[1], q1.at[X + 1], hs1.at[0], hr1.at[1], "stream", st - 1).start()

    @pl.when(inner_r)
    def _():
        remote(q1.at[X], q1.at[0], hs1.at[1], hr1.at[0], "stream", st + 1).start()

    @pl.when(inner_l)
    def _():
        arrived(q1.at[0], hr1.at[0])

    @pl.when(inner_r)
    def _():
        arrived(q1.at[X + 1], hr1.at[1])

    def chunk(j):
        wait_chunk(j)
        before, now = done_after(j - 1), done_after(j)
        loop(before, now, sweep1)
        loop(jnp.where(j == 1, 0, before - 2), jnp.where(j == CHUNKS - 1, X, now - 2), sweep2)

    loop(1, CHUNKS, chunk)

    part = jnp.sum(wall[...] * gv[...], axis=0, keepdims=True)
    sum1[me] = jnp.broadcast_to(part, (8, 128))
    for phase, (axis, pos, buf) in enumerate((("span", me, sum1), ("stream", st, sum2))):

        def one(i):
            remote(buf.at[pos], buf.at[pos], ps.at[phase], pr.at[phase], axis, lax.rem(pos + i, 16)).start()

        loop(1, 16, one)
        arrived(buf.at[pl.ds(0, 15)], pr.at[phase])
        total = buf[0]
        for i in range(1, 16):
            total = total + buf[i]
        if phase == 0:
            sum2[st] = total
    scale = 1.0 / math.sqrt(256 * 128)
    group = lax.div(lax.broadcasted_iota(jnp.int32, (1, 128), 1), X)
    for m in range(2):
        for r in range(2):
            forces[m, r] = jnp.sum(jnp.where(group == 2 * m + r, total[0:1], 0.0)) * scale

    for phase, buf in enumerate((sum1, sum2)):
        arrived(buf.at[pl.ds(0, 15)], ps.at[phase])
    arrived(fv.at[pl.ds(0, S - 1)], fs.at[0])
    arrived(mv.at[pl.ds(0, S - 1)], fs.at[1])
    arrived(fbuf.at[:, pl.ds(0, NZ - Z), :], send1)
    arrived(sbuf.at[:, pl.ds(0, NZ - Z), :], send2)

    @pl.when(inner_l)
    def _():
        arrived(q0.at[0], hs0.at[0])
        arrived(q1.at[0], hs1.at[0])

    @pl.when(inner_r)
    def _():
        arrived(q0.at[0], hs0.at[1])
        arrived(q1.at[0], hs1.at[1])

    arrived(q2, osem)


def shards(forcing, initial_state, diagonal, span_speed, coupling, stiffener_mask, face_index, mode_shapes):
    high, low = table_rows()
    anyw = pl.BlockSpec(memory_space=pl.ANY)
    smem = pl.BlockSpec(memory_space=pltpu.SMEM)
    vm = pltpu.VMEM
    dma = pltpu.SemaphoreType.DMA
    flow, forces = pl.pallas_call(
        kernel,
        out_shape=(
            jax.ShapeDtypeStruct((K, C, 2, X, 1, Y), f32),
            jax.ShapeDtypeStruct((2, 2), f32),
        ),
        in_specs=[anyw, anyw, anyw, smem, smem, anyw, anyw, anyw, anyw, anyw],
        out_specs=(anyw, smem),
        scratch_shapes=[
            vm((NZ, NZ), bf16), vm((NZ, NZ), bf16),
            vm((CHUNKS, NZ, Y), f32), vm((CHUNKS, NZ, Y), f32),
            vm((X, C, KR, Y), f32),
            vm((X + 2, C, KR, Y), f32), vm((X + 2, C, KR, Y), f32), vm((X, C, KR, Y), f32),
            vm((X, C, KR, Y), f32),
            vm((X, C, K, Y), f32), vm((X, C, K, Y), f32),
            vm((100, 8, Y), f32),
            vm((C, X, Y), f32), vm((X, Y), jnp.int32), vm((C, K, Y), f32),
            vm((S, 2, 128), jnp.int32), vm((S, 2, 2, 128), f32),
            vm((NZ, 128), f32), vm((KR, 128), f32), vm((KR, 128), f32),
            vm((16, 8, 128), f32), vm((16, 8, 128), f32),
            vm((2, 128), jnp.int32), vm((2, 2, 128), f32),
            dma((2,)), dma, dma((2,)), dma((2,)),
            dma, dma((CHUNKS,)), dma, dma((CHUNKS,)),
            dma((2,)), dma((2,)), dma((2,)), dma((2,)),
            dma((2,)), dma((2,)), dma((2,)), dma((2,)), dma,
        ],
        compiler_params=pltpu.CompilerParams(
            collective_id=0, has_side_effects=True, vmem_limit_bytes=64 * 1024 * 1000
        ),
    )(
        forcing.reshape(C, Z, X, 1, Y),
        initial_state.reshape(K, C, 2, X, 1, Y),
        diagonal, span_speed, coupling, stiffener_mask, face_index, mode_shapes,
        jnp.asarray(high), jnp.asarray(low),
    )
    return flow.reshape(K, C, 2, X, Y), forces


def solution(mesh):
    return jax.shard_map(
        shards,
        mesh=mesh,
        in_specs=(
            P(None, "span", "stream", None),
            P("span", None, None, "stream", None),
            P(),
            P(),
            P(),
            P(),
            P(None, ("stream", "span")),
            P(None, None, ("stream", "span")),
        ),
        out_specs=(P("span", None, None, "stream", None), P()),
        check_vma=False,
    )
```

```python
import functools
import math

import jax
import jax.numpy as jnp
import numpy as np
from jax import lax
from jax.experimental import pallas as pl
from jax.experimental.pallas import tpu as pltpu
from jax.sharding import PartitionSpec as P

MESH = pl.DeviceIdType.MESH
S = 16
N = 16
K = 16
C = 5
X = 32
Z = 32
Y = 128
NZ = 512
KR = 2 * K
CHUNKS = X * C // S
HELD = 7
EARLY = 2
MIDDLE = 6
f32 = jnp.float32
bf16 = jnp.bfloat16


def table_rows():
    z = np.arange(NZ)
    k = np.arange(NZ // 2)
    phase = (k[:, None] * z[None, :] % NZ) * (2.0 * math.pi / NZ)
    both = np.stack([np.cos(phase), -np.sin(phase)], 0) / math.sqrt(NZ)
    rows = both.reshape(2, S, K, NZ).transpose(1, 0, 2, 3).reshape(NZ, NZ)
    exact = rows.astype(np.float32)
    high = exact.astype(jnp.bfloat16)
    low = (exact - high.astype(np.float32)).astype(jnp.bfloat16)
    return high, low


def split(v):
    high = v.astype(bf16)
    return high, (v - high.astype(f32)).astype(bf16)


def dot3(ah, al, bh, bl):
    d = functools.partial(jnp.dot, preferred_element_type=f32)
    return d(ah, bh) + (d(ah, bl) + d(al, bh))


def cell(order):
    half = lax.div(order, 2)
    return jnp.where(lax.rem(order, 2) == 0, half, X - 1 - half)


def row_of(j, p):
    rho = j * S + p
    return cell(lax.div(rho, C)), lax.rem(rho, C)


def done_after(j):
    return lax.div((j + 1) * S, C)


def loop(lo, hi, body):
    def step(i, carry):
        body(i)
        return carry

    lax.fori_loop(lo, hi, step, 0)


def kernel(
    forcing, init, diag, speed, coup, mask, faces, modes, thigh, tlow,
    flow, forces,
    th, tl, fbuf, sbuf, rhs, q0, q1, q2, near0, alpha, beta, coef, dv, kv, bv,
    fv, mv, wallm, gv, wall, sum1, sum2, fown, mown,
    wsend, wrecv, rhsw, q1w,
    sem_t, sem_q, sem_d, sem_f, send1, recv1, send2, recv2,
    hs0, hr0, hs1, hr1, hs2, hr2, ws, wr, fs, fr, ps, pr, osem,
):
    me = lax.axis_index("span")
    st = lax.axis_index("stream")
    first, last = st == 0, st == N - 1
    inner_l, inner_r = st > 0, st < N - 1

    def remote(src, dst, ss, rs, axis, to):
        return pltpu.make_async_remote_copy(
            src_ref=src, dst_ref=dst, send_sem=ss, recv_sem=rs, device_id={axis: to}, device_id_type=MESH
        )

    def arrived(ref, sem):
        pltpu.make_async_copy(ref, ref, sem).wait()

    barrier = pltpu.get_barrier_semaphore()

    def greet(i):
        pl.semaphore_signal(barrier, inc=1, device_id={"span": lax.rem(me + i, S)}, device_id_type=MESH)
        pl.semaphore_signal(barrier, inc=1, device_id={"stream": lax.rem(st + i, N)}, device_id_type=MESH)

    loop(1, S, greet)

    x0 = pl.multiple_of(st * X, X)
    cp_d = pltpu.make_async_copy(diag.at[:, pl.ds(x0, X), :], dv, sem_d.at[0])
    cp_k = pltpu.make_async_copy(mask.at[pl.ds(x0, X), :], kv, sem_d.at[1])
    cp_d.start()
    cp_k.start()
    cp_h = pltpu.make_async_copy(thigh, th, sem_t.at[0])
    cp_l = pltpu.make_async_copy(tlow, tl, sem_t.at[1])
    cp_h.start()
    cp_l.start()
    cp_f = pltpu.make_async_copy(faces, fown, sem_f.at[0])
    cp_m = pltpu.make_async_copy(modes, mown, sem_f.at[1])
    cp_f.start()
    cp_m.start()

    mine = pl.multiple_of(me * Z, Z)

    def own_rows(j):
        x, c = row_of(j, me)
        pltpu.make_async_copy(forcing.at[c, :, x, 0, :], fbuf.at[j, pl.ds(mine, Z), :], recv1.at[j]).start()

    loop(0, CHUNKS, own_rows)

    def load_state(x):
        for c in range(C):
            for r in range(2):
                pltpu.make_async_copy(
                    init.at[:, c, r, x, 0, :], q0.at[x + 1, c, pl.ds(r * K, K), :], sem_q
                ).start()

    loop(0, X, load_state)

    for a in range(4):
        for c in range(C):
            for d in range(C):
                coef[a * 25 + c * 5 + d] = jnp.full((8, Y), coup[c, a, d], f32)
    k_index = (me * K + lax.broadcasted_iota(jnp.int32, (K, Y), 0)).astype(f32)
    for c in range(C):
        bv[c] = k_index * (2.0 * math.pi / NZ) * speed[c]

    @pl.when(first)
    def _():
        q0[0] = jnp.zeros((C, KR, Y), f32)
        q1[0] = jnp.zeros((C, KR, Y), f32)
        q1w[0] = jnp.zeros((C, KR, Y), f32)

    @pl.when(last)
    def _():
        q0[X + 1] = jnp.zeros((C, KR, Y), f32)
        q1[X + 1] = jnp.zeros((C, KR, Y), f32)
        q1w[X + 1] = jnp.zeros((C, KR, Y), f32)

    cp_f.wait()
    cp_m.wait()
    fv[me] = fown[...]
    mv[me] = mown[...]
    pl.semaphore_wait(barrier, 2 * S - 2)

    def halo0(c):
        for r in range(2):
            rows = pl.ds(r * K, K)

            @pl.when(inner_l)
            def _():
                remote(init.at[:, c, r, 0, 0, :], q0.at[X + 1, c, rows, :], hs0.at[0], hr0.at[1], "stream", st - 1).start()

            @pl.when(inner_r)
            def _():
                remote(init.at[:, c, r, X - 1, 0, :], q0.at[0, c, rows, :], hs0.at[1], hr0.at[0], "stream", st + 1).start()

    loop(0, C, halo0)

    def send_forcing(j):
        def one(i):
            t = lax.rem(me + i, S)
            x, c = row_of(j, t)
            remote(
                forcing.at[c, :, x, 0, :], fbuf.at[j, pl.ds(mine, Z), :], send1, recv1.at[j], "span", t
            ).start()

        loop(1, S, one)

    def send_faces(i):
        t = lax.rem(me + i, S)
        remote(fown, fv.at[me], fs.at[0], fr.at[0], "span", t).start()
        remote(mown, mv.at[me], fs.at[1], fr.at[1], "span", t).start()

    send_forcing(0)
    loop(1, S, send_faces)
    loop(1, CHUNKS, send_forcing)

    cp_d.wait()
    cp_k.wait()

    def factors(x):
        keep = 1.0 - kv[pl.ds(x, 1), :].astype(f32)
        for c in range(C):
            a = jnp.broadcast_to(dv[c, pl.ds(x, 1), :], (K, Y))
            b = bv[c]
            scale = keep / (a * a + b * b)
            alpha[x, c] = a * scale
            beta[x, c] = b * scale

    loop(0, X, factors)

    lane = lax.broadcasted_iota(jnp.int32, (KR, Y), 1)

    def near(q, x, outs=tuple(range(C))):
        acc = [None] * len(outs)
        for d in range(C):
            here = q[x + 1, d]
            up = jnp.where(lane < Y - 1, pltpu.roll(here, Y - 1, 1), 0.0)
            down = jnp.where(lane > 0, pltpu.roll(here, 1, 1), 0.0)
            for a, v in enumerate((q[x + 2, d], q[x, d], up, down)):
                v = v.reshape(4, 8, Y)
                for i, c in enumerate(outs):
                    term = coef[a * 25 + c * 5 + d][None] * v
                    acc[i] = term if acc[i] is None else acc[i] + term
        return [v.reshape(KR, Y) for v in acc]

    arrived(q0.at[pl.ds(1, X)], sem_q)

    @pl.when(inner_l)
    def _():
        arrived(q0.at[0], hr0.at[0])

    @pl.when(inner_r)
    def _():
        arrived(q0.at[X + 1], hr0.at[1])

    def first_near(x):
        for c, v in enumerate(near(q0, x)):
            near0[x, c] = v

    loop(0, X, first_near)

    cp_h.wait()
    cp_l.wait()

    def transform(j):
        arrived(fbuf.at[j], recv1.at[j])
        fh, fl = split(fbuf[j])
        for i in range(4):
            part = pl.ds(i * 128, 128)
            value = dot3(th[part, :], tl[part, :], fh, fl)
            sbuf[j, part, :] = value
            value = value.reshape(4, 4, 8, Y)
            for g in range(4):
                moved = pltpu.roll(value[:, g].reshape(KR, Y), X * g + 2 * j, 1)
                kept = jnp.where(lax.div(lane, 2) == 16 * g + j, moved, 0.0)
                wsend[pl.ds(4 * i, 4)] += kept.reshape(4, 8, Y)
        x, c = row_of(j, me)
        rhs[x, c] = sbuf[j, pl.ds(mine, KR), :]

    def send_rows(j):
        x, c = row_of(j, me)

        def one(i):
            t = lax.rem(me + i, S)
            rows_t = pl.ds(pl.multiple_of(t * KR, KR), KR)
            remote(sbuf.at[j, rows_t, :], rhs.at[x, c], send2, recv2.at[j], "span", t).start()

        loop(1, S, one)

    wsend[...] = jnp.zeros((S, 8, Y), f32)
    loop(0, HELD, transform)
    loop(0, EARLY, send_rows)
    loop(HELD, CHUNKS, transform)
    wrecv[me] = wsend[me]

    def send_wall(i):
        t = lax.rem(me + i, S)
        remote(wsend.at[t], wrecv.at[me], ws, wr, "span", t).start()

    loop(1, S, send_wall)
    loop(EARLY, MIDDLE, send_rows)

    arrived(fv.at[pl.ds(0, S - 1)], fr.at[0])
    arrived(mv.at[pl.ds(0, S - 1)], fr.at[1])
    z_row = lax.broadcasted_iota(jnp.int32, (Z, 128), 0)
    x_row = lax.broadcasted_iota(jnp.int32, (128, 128), 0)

    def scatter(s):
        total = jnp.zeros((Z, 128), f32)
        for m in range(2):
            index = fv[s, pl.ds(m, 1), :]
            at_z = z_row == lax.div(index, X)
            for r in range(2):
                placed = (x_row == lax.rem(index, X) + (2 * m + r) * X).astype(f32)
                value = jnp.where(at_z, mv[s, m, pl.ds(r, 1), :], 0.0)
                total = total + lax.dot_general(
                    value, placed, (((1,), (1,)), ((), ())),
                    precision=lax.Precision.HIGHEST, preferred_element_type=f32,
                )
        wallm[pl.ds(pl.multiple_of(s * Z, Z), Z), :] = total

    loop(0, S, scatter)
    wh, wl = split(wallm[...])
    own_k = pl.ds(pl.multiple_of(me * KR, KR), KR)
    row = lax.broadcasted_iota(jnp.int32, (KR, Y), 0)
    zero_k = jnp.logical_and(me == 0, lax.rem(row, K) == 0)
    weight = jnp.where(zero_k, 1.0, 2.0)
    gv[...] = weight * dot3(th[own_k, :], tl[own_k, :], wh, wl)
    wall[...] = jnp.zeros((KR, 128), f32)

    def invert(x, c, d):
        re, im = d[:K], d[K:]
        al, be = alpha[x, c], beta[x, c]
        return al * re + be * im, al * im - be * re

    def sweep1(order):
        x = cell(order)
        for c in range(C):
            re, im = invert(x, c, rhs[x, c] - near0[x, c])
            q1[x + 1, c, 0:K] = re
            q1[x + 1, c, K:KR] = im

    def sweep2(order):
        x = cell(order)
        for c, v in enumerate(near(q1, x)):
            re, im = invert(x, c, rhs[x, c] - v)
            q2[x, c, 0:K] = re
            q2[x, c, K:KR] = im
        for c in range(C):
            for r in range(2):
                pltpu.make_async_copy(
                    q2.at[x, c, pl.ds(r * K, K), :], flow.at[:, c, r, x, 0, :], osem
                ).start()

    def halos(q, hs, hr):
        @pl.when(inner_l)
        def _():
            remote(q.at[1], q.at[X + 1], hs.at[0], hr.at[1], "stream", st - 1).start()

        @pl.when(inner_r)
        def _():
            remote(q.at[X], q.at[0], hs.at[1], hr.at[0], "stream", st + 1).start()

        @pl.when(inner_l)
        def _():
            arrived(q.at[0], hr.at[0])

        @pl.when(inner_r)
        def _():
            arrived(q.at[X + 1], hr.at[1])

    arrived(wrecv.at[pl.ds(0, S - 1)], wr)

    def unpack(p):
        tile = wrecv[p]
        for j in range(CHUNKS):
            x, c = row_of(j, p)
            for g in range(4):
                rhsw[x, c, 8 * g : 8 * g + 8] = pltpu.roll(tile, (Y - X * g - 2 * j) % Y, 1)
            re, im = invert(x, c, rhsw[x, c] - near0[x, c])
            q1w[x + 1, c, 0:K] = re
            q1w[x + 1, c, K:KR] = im

    loop(0, S, unpack)
    halos(q1w, hs2, hr2)

    def wall_values(x):
        (v,) = near(q1w, x, (C - 1,))
        re, im = invert(x, C - 1, rhsw[x, C - 1] - v)
        at = jnp.concatenate([re, im], 0)[:, 0:1]
        wall[...] += jnp.where(lax.rem(lane, X) == x, at, 0.0)

    loop(0, X, wall_values)
    part = jnp.sum(wall[...] * gv[...], axis=0, keepdims=True)

    def start_sum(phase, axis, pos, buf):
        def one(i):
            remote(buf.at[pos], buf.at[pos], ps.at[phase], pr.at[phase], axis, lax.rem(pos + i, 16)).start()

        loop(1, 16, one)

    def end_sum(phase, buf):
        arrived(buf.at[pl.ds(0, 15)], pr.at[phase])
        total = buf[0]
        for i in range(1, 16):
            total = total + buf[i]
        return total

    sum1[me] = jnp.broadcast_to(part, (8, 128))
    start_sum(0, "span", me, sum1)
    loop(MIDDLE, CHUNKS, send_rows)

    def wait_chunk(j):
        pltpu.make_async_copy(rhs.at[pl.ds(0, 3)], rhs.at[pl.ds(0, 3)], recv2.at[j]).wait()

    wait_chunk(0)
    loop(0, S // C, sweep1)

    halos(q1, hs1, hr1)

    def chunk(j):
        wait_chunk(j)
        before, now = done_after(j - 1), done_after(j)
        loop(before, now, sweep1)
        loop(jnp.where(j == 1, 0, before - 2), jnp.where(j == CHUNKS - 1, X, now - 2), sweep2)

    loop(1, 6, chunk)
    sum2[st] = end_sum(0, sum1)
    start_sum(1, "stream", st, sum2)
    loop(6, 8, chunk)
    total = end_sum(1, sum2)
    scale = 1.0 / math.sqrt(256 * 128)
    group = lax.div(lax.broadcasted_iota(jnp.int32, (1, 128), 1), X)
    for m in range(2):
        for r in range(2):
            forces[m, r] = jnp.sum(jnp.where(group == 2 * m + r, total[0:1], 0.0)) * scale

    loop(8, CHUNKS, chunk)

    for phase, buf in enumerate((sum1, sum2)):
        arrived(buf.at[pl.ds(0, 15)], ps.at[phase])
    arrived(wsend.at[pl.ds(0, S - 1)], ws)
    arrived(fv.at[pl.ds(0, S - 1)], fs.at[0])
    arrived(mv.at[pl.ds(0, S - 1)], fs.at[1])
    arrived(fbuf.at[:, pl.ds(0, NZ - Z), :], send1)
    arrived(sbuf.at[:, pl.ds(0, NZ - Z), :], send2)

    @pl.when(inner_l)
    def _():
        arrived(q0.at[0], hs0.at[0])
        arrived(q1.at[0], hs1.at[0])
        arrived(q1.at[0], hs2.at[0])

    @pl.when(inner_r)
    def _():
        arrived(q0.at[0], hs0.at[1])
        arrived(q1.at[0], hs1.at[1])
        arrived(q1.at[0], hs2.at[1])

    arrived(q2, osem)


def shards(forcing, initial_state, diagonal, span_speed, coupling, stiffener_mask, face_index, mode_shapes):
    high, low = table_rows()
    anyw = pl.BlockSpec(memory_space=pl.ANY)
    smem = pl.BlockSpec(memory_space=pltpu.SMEM)
    vm = pltpu.VMEM
    dma = pltpu.SemaphoreType.DMA
    flow, forces = pl.pallas_call(
        kernel,
        out_shape=(
            pltpu.VMEM((K, C, 2, X, 1, Y), f32),
            jax.ShapeDtypeStruct((2, 2), f32),
        ),
        in_specs=[anyw, anyw, anyw, smem, smem, anyw, anyw, anyw, anyw, anyw],
        out_specs=(pl.BlockSpec(memory_space=pltpu.VMEM), smem),
        scratch_shapes=[
            vm((NZ, NZ), bf16), vm((NZ, NZ), bf16),
            vm((CHUNKS, NZ, Y), f32), vm((CHUNKS, NZ, Y), f32),
            vm((X, C, KR, Y), f32),
            vm((X + 2, C, KR, Y), f32), vm((X + 2, C, KR, Y), f32), vm((X, C, KR, Y), f32),
            vm((X, C, KR, Y), f32),
            vm((X, C, K, Y), f32), vm((X, C, K, Y), f32),
            vm((100, 8, Y), f32),
            vm((C, X, Y), f32), vm((X, Y), jnp.int32), vm((C, K, Y), f32),
            vm((S, 2, 128), jnp.int32), vm((S, 2, 2, 128), f32),
            vm((NZ, 128), f32), vm((KR, 128), f32), vm((KR, 128), f32),
            vm((16, 8, 128), f32), vm((16, 8, 128), f32),
            vm((2, 128), jnp.int32), vm((2, 2, 128), f32),
            vm((S, 8, Y), f32), vm((S, 8, Y), f32), vm((X, C, KR, Y), f32), vm((X + 2, C, KR, Y), f32),
            dma((2,)), dma, dma((2,)), dma((2,)),
            dma, dma((CHUNKS,)), dma, dma((CHUNKS,)),
            dma((2,)), dma((2,)), dma((2,)), dma((2,)), dma((2,)), dma((2,)), dma, dma,
            dma((2,)), dma((2,)), dma((2,)), dma((2,)), dma,
        ],
        compiler_params=pltpu.CompilerParams(
            collective_id=0, has_side_effects=True, vmem_limit_bytes=64_350_000
        ),
    )(
        forcing.reshape(C, Z, X, 1, Y),
        initial_state.reshape(K, C, 2, X, 1, Y),
        diagonal, span_speed, coupling.transpose(1, 0, 2), stiffener_mask, face_index, mode_shapes,
        jnp.asarray(high), jnp.asarray(low),
    )
    return flow.reshape(K, C, 2, X, Y), forces


def solution(mesh):
    return jax.shard_map(
        shards,
        mesh=mesh,
        in_specs=(
            P(None, "span", "stream", None),
            P("span", None, None, "stream", None),
            P(),
            P(),
            P(),
            P(),
            P(None, ("stream", "span")),
            P(None, None, ("stream", "span")),
        ),
        out_specs=(P("span", None, None, "stream", None), P()),
        check_vma=False,
    )
```

```python
import functools
import math

import jax
import jax.numpy as jnp
import numpy as np
from jax import lax
from jax.experimental import pallas as pl
from jax.experimental.pallas import tpu as pltpu
from jax.sharding import PartitionSpec as P

MESH = pl.DeviceIdType.MESH
S = 16
N = 16
K = 16
C = 5
X = 32
Z = 32
Y = 128
NZ = 512
KR = 2 * K
CHUNKS = X * C // S
HELD = 7
EARLY = 2
MIDDLE = 6
f32 = jnp.float32
bf16 = jnp.bfloat16


def table_rows():
    z = np.arange(NZ)
    k = np.arange(NZ // 2)
    phase = (k[:, None] * z[None, :] % NZ) * (2.0 * math.pi / NZ)
    both = np.stack([np.cos(phase), -np.sin(phase)], 0) / math.sqrt(NZ)
    rows = both.reshape(2, S, K, NZ).transpose(1, 0, 2, 3).reshape(NZ, NZ)
    exact = rows.astype(np.float32)
    high = exact.astype(jnp.bfloat16)
    low = (exact - high.astype(np.float32)).astype(jnp.bfloat16)
    return high, low


def split(v):
    high = v.astype(bf16)
    return high, (v - high.astype(f32)).astype(bf16)


def dot3(ah, al, bh, bl):
    d = functools.partial(jnp.dot, preferred_element_type=f32)
    return d(ah, bh) + (d(ah, bl) + d(al, bh))


def cell(order):
    half = lax.div(order, 2)
    return jnp.where(lax.rem(order, 2) == 0, half, X - 1 - half)


def row_of(j, p):
    rho = j * S + p
    return cell(lax.div(rho, C)), lax.rem(rho, C)


def done_after(j):
    return lax.div((j + 1) * S, C)


def far_first(i):
    half = lax.div(i + 1, 2)
    return jnp.where(lax.rem(i, 2) == 1, S // 2 - half, S // 2 + half)


def loop(lo, hi, body):
    def step(i, carry):
        body(i)
        return carry

    lax.fori_loop(lo, hi, step, 0)


def kernel(
    forcing, init, diag, speed, coup, mask, faces, modes, thigh, tlow,
    flow, forces,
    th, tl, fbuf, sbuf, rhs, q0, q1, q2, near0, alpha, beta, coef, dv, kv, bv,
    fv, mv, wallm, gv, wall, sum1, sum2, fown, mown,
    wsend, wrecv, rhsw, q1w,
    sem_t, sem_q, sem_d, sem_f, send1, recv1, send2, recv2,
    hs0, hr0, hs1, hr1, hs2, hr2, ws, wr, fs, fr, ps, pr, osem,
):
    me = lax.axis_index("span")
    st = lax.axis_index("stream")
    first, last = st == 0, st == N - 1
    inner_l, inner_r = st > 0, st < N - 1

    def remote(src, dst, ss, rs, axis, to):
        return pltpu.make_async_remote_copy(
            src_ref=src, dst_ref=dst, send_sem=ss, recv_sem=rs, device_id={axis: to}, device_id_type=MESH
        )

    def arrived(ref, sem):
        pltpu.make_async_copy(ref, ref, sem).wait()

    barrier = pltpu.get_barrier_semaphore()

    def greet(i):
        pl.semaphore_signal(barrier, inc=1, device_id={"span": lax.rem(me + i, S)}, device_id_type=MESH)
        pl.semaphore_signal(barrier, inc=1, device_id={"stream": lax.rem(st + i, N)}, device_id_type=MESH)

    loop(1, S, greet)

    x0 = pl.multiple_of(st * X, X)
    cp_d = pltpu.make_async_copy(diag.at[:, pl.ds(x0, X), :], dv, sem_d.at[0])
    cp_k = pltpu.make_async_copy(mask.at[pl.ds(x0, X), :], kv, sem_d.at[1])
    cp_d.start()
    cp_k.start()
    cp_h = pltpu.make_async_copy(thigh, th, sem_t.at[0])
    cp_l = pltpu.make_async_copy(tlow, tl, sem_t.at[1])
    cp_h.start()
    cp_l.start()
    cp_f = pltpu.make_async_copy(faces, fown, sem_f.at[0])
    cp_m = pltpu.make_async_copy(modes, mown, sem_f.at[1])
    cp_f.start()
    cp_m.start()

    mine = pl.multiple_of(me * Z, Z)

    def own_rows(j):
        x, c = row_of(j, me)
        pltpu.make_async_copy(forcing.at[c, :, x, 0, :], fbuf.at[j, pl.ds(mine, Z), :], recv1.at[j]).start()

    loop(0, CHUNKS, own_rows)

    def load_state(x):
        for c in range(C):
            for r in range(2):
                pltpu.make_async_copy(
                    init.at[:, c, r, x, 0, :], q0.at[x + 1, c, pl.ds(r * K, K), :], sem_q
                ).start()

    loop(0, X, load_state)

    for a in range(4):
        for c in range(C):
            for d in range(C):
                coef[a * 25 + c * 5 + d] = jnp.full((8, Y), coup[c, a, d], f32)
    k_index = (me * K + lax.broadcasted_iota(jnp.int32, (K, Y), 0)).astype(f32)
    for c in range(C):
        bv[c] = k_index * (2.0 * math.pi / NZ) * speed[c]

    @pl.when(first)
    def _():
        q0[0] = jnp.zeros((C, KR, Y), f32)
        q1[0] = jnp.zeros((C, KR, Y), f32)
        q1w[0] = jnp.zeros((C, KR, Y), f32)

    @pl.when(last)
    def _():
        q0[X + 1] = jnp.zeros((C, KR, Y), f32)
        q1[X + 1] = jnp.zeros((C, KR, Y), f32)
        q1w[X + 1] = jnp.zeros((C, KR, Y), f32)

    cp_f.wait()
    cp_m.wait()
    fv[me] = fown[...]
    mv[me] = mown[...]
    pl.semaphore_wait(barrier, 2 * S - 2)

    def halo0(c):
        for r in range(2):
            rows = pl.ds(r * K, K)

            @pl.when(inner_l)
            def _():
                remote(init.at[:, c, r, 0, 0, :], q0.at[X + 1, c, rows, :], hs0.at[0], hr0.at[1], "stream", st - 1).start()

            @pl.when(inner_r)
            def _():
                remote(init.at[:, c, r, X - 1, 0, :], q0.at[0, c, rows, :], hs0.at[1], hr0.at[0], "stream", st + 1).start()

    loop(0, C, halo0)

    def send_forcing(j):
        def one(i):
            t = lax.rem(me + i, S)
            x, c = row_of(j, t)
            remote(
                forcing.at[c, :, x, 0, :], fbuf.at[j, pl.ds(mine, Z), :], send1, recv1.at[j], "span", t
            ).start()

        loop(1, S, one)

    def send_faces(i):
        t = lax.rem(me + i, S)
        remote(fown, fv.at[me], fs.at[0], fr.at[0], "span", t).start()
        remote(mown, mv.at[me], fs.at[1], fr.at[1], "span", t).start()

    send_forcing(0)
    loop(1, S, send_faces)
    loop(1, CHUNKS, send_forcing)

    cp_d.wait()
    cp_k.wait()

    def factors(x):
        keep = 1.0 - kv[pl.ds(x, 1), :].astype(f32)
        for c in range(C):
            a = jnp.broadcast_to(dv[c, pl.ds(x, 1), :], (K, Y))
            b = bv[c]
            scale = keep / (a * a + b * b)
            alpha[x, c] = a * scale
            beta[x, c] = b * scale

    loop(0, X, factors)

    lane = lax.broadcasted_iota(jnp.int32, (KR, Y), 1)

    def near(q, x, outs=tuple(range(C))):
        acc = [None] * len(outs)
        for d in range(C):
            here = q[x + 1, d]
            up = jnp.where(lane < Y - 1, pltpu.roll(here, Y - 1, 1), 0.0)
            down = jnp.where(lane > 0, pltpu.roll(here, 1, 1), 0.0)
            for a, v in enumerate((q[x + 2, d], q[x, d], up, down)):
                v = v.reshape(4, 8, Y)
                for i, c in enumerate(outs):
                    term = coef[a * 25 + c * 5 + d][None] * v
                    acc[i] = term if acc[i] is None else acc[i] + term
        return [v.reshape(KR, Y) for v in acc]

    arrived(q0.at[pl.ds(1, X)], sem_q)

    @pl.when(inner_l)
    def _():
        arrived(q0.at[0], hr0.at[0])

    @pl.when(inner_r)
    def _():
        arrived(q0.at[X + 1], hr0.at[1])

    def first_near(x):
        for c, v in enumerate(near(q0, x)):
            near0[x, c] = v

    loop(0, X, first_near)

    cp_h.wait()
    cp_l.wait()

    def transform(j):
        arrived(fbuf.at[j], recv1.at[j])
        fh, fl = split(fbuf[j])
        for i in range(4):
            part = pl.ds(i * 128, 128)
            value = dot3(th[part, :], tl[part, :], fh, fl)
            sbuf[j, part, :] = value
            value = value.reshape(4, 4, 8, Y)
            for g in range(4):
                moved = pltpu.roll(value[:, g].reshape(KR, Y), X * g + 2 * j, 1)
                kept = jnp.where(lax.div(lane, 2) == 16 * g + j, moved, 0.0)
                wsend[pl.ds(4 * i, 4)] += kept.reshape(4, 8, Y)
        x, c = row_of(j, me)
        rhs[x, c] = sbuf[j, pl.ds(mine, KR), :]

    def send_rows(j):
        x, c = row_of(j, me)

        def one(i):
            t = lax.rem(me + far_first(i), S)
            rows_t = pl.ds(pl.multiple_of(t * KR, KR), KR)
            remote(sbuf.at[j, rows_t, :], rhs.at[x, c], send2, recv2.at[j], "span", t).start()

        loop(0, S - 1, one)

    wsend[...] = jnp.zeros((S, 8, Y), f32)
    loop(0, HELD, transform)
    loop(0, EARLY, send_rows)
    loop(HELD, CHUNKS, transform)
    wrecv[me] = wsend[me]

    def send_wall(i):
        t = lax.rem(me + i, S)
        remote(wsend.at[t], wrecv.at[me], ws, wr, "span", t).start()

    loop(1, S, send_wall)
    loop(EARLY, MIDDLE, send_rows)

    arrived(fv.at[pl.ds(0, S - 1)], fr.at[0])
    arrived(mv.at[pl.ds(0, S - 1)], fr.at[1])
    z_row = lax.broadcasted_iota(jnp.int32, (Z, 128), 0)
    x_row = lax.broadcasted_iota(jnp.int32, (128, 128), 0)

    def scatter(s):
        total = jnp.zeros((Z, 128), f32)
        for m in range(2):
            index = fv[s, pl.ds(m, 1), :]
            at_z = z_row == lax.div(index, X)
            for r in range(2):
                placed = (x_row == lax.rem(index, X) + (2 * m + r) * X).astype(f32)
                value = jnp.where(at_z, mv[s, m, pl.ds(r, 1), :], 0.0)
                total = total + lax.dot_general(
                    value, placed, (((1,), (1,)), ((), ())),
                    precision=lax.Precision.HIGHEST, preferred_element_type=f32,
                )
        wallm[pl.ds(pl.multiple_of(s * Z, Z), Z), :] = total

    loop(0, S, scatter)
    wh, wl = split(wallm[...])
    own_k = pl.ds(pl.multiple_of(me * KR, KR), KR)
    row = lax.broadcasted_iota(jnp.int32, (KR, Y), 0)
    zero_k = jnp.logical_and(me == 0, lax.rem(row, K) == 0)
    weight = jnp.where(zero_k, 1.0, 2.0)
    gv[...] = weight * dot3(th[own_k, :], tl[own_k, :], wh, wl)
    wall[...] = jnp.zeros((KR, 128), f32)

    def invert(x, c, d):
        re, im = d[:K], d[K:]
        al, be = alpha[x, c], beta[x, c]
        return al * re + be * im, al * im - be * re

    def sweep1(order):
        x = cell(order)
        for c in range(C):
            re, im = invert(x, c, rhs[x, c] - near0[x, c])
            q1[x + 1, c, 0:K] = re
            q1[x + 1, c, K:KR] = im

    def sweep2(order):
        x = cell(order)
        for c, v in enumerate(near(q1, x)):
            re, im = invert(x, c, rhs[x, c] - v)
            q2[x, c, 0:K] = re
            q2[x, c, K:KR] = im
        for c in range(C):
            for r in range(2):
                pltpu.make_async_copy(
                    q2.at[x, c, pl.ds(r * K, K), :], flow.at[:, c, r, x, 0, :], osem
                ).start()

    def halos(q, hs, hr):
        @pl.when(inner_l)
        def _():
            remote(q.at[1], q.at[X + 1], hs.at[0], hr.at[1], "stream", st - 1).start()

        @pl.when(inner_r)
        def _():
            remote(q.at[X], q.at[0], hs.at[1], hr.at[0], "stream", st + 1).start()

        @pl.when(inner_l)
        def _():
            arrived(q.at[0], hr.at[0])

        @pl.when(inner_r)
        def _():
            arrived(q.at[X + 1], hr.at[1])

    arrived(wrecv.at[pl.ds(0, S - 1)], wr)

    def unpack(p):
        tile = wrecv[p]
        for j in range(CHUNKS):
            x, c = row_of(j, p)
            for g in range(4):
                rhsw[x, c, 8 * g : 8 * g + 8] = pltpu.roll(tile, (Y - X * g - 2 * j) % Y, 1)
            re, im = invert(x, c, rhsw[x, c] - near0[x, c])
            q1w[x + 1, c, 0:K] = re
            q1w[x + 1, c, K:KR] = im

    loop(0, S, unpack)
    halos(q1w, hs2, hr2)

    def wall_values(x):
        (v,) = near(q1w, x, (C - 1,))
        re, im = invert(x, C - 1, rhsw[x, C - 1] - v)
        at = jnp.concatenate([re, im], 0)[:, 0:1]
        wall[...] += jnp.where(lax.rem(lane, X) == x, at, 0.0)

    loop(0, X, wall_values)
    part = jnp.sum(wall[...] * gv[...], axis=0, keepdims=True)

    def start_sum(phase, axis, pos, buf):
        def one(i):
            remote(buf.at[pos], buf.at[pos], ps.at[phase], pr.at[phase], axis, lax.rem(pos + i, 16)).start()

        loop(1, 16, one)

    def end_sum(phase, buf):
        arrived(buf.at[pl.ds(0, 15)], pr.at[phase])
        total = buf[0]
        for i in range(1, 16):
            total = total + buf[i]
        return total

    sum1[me] = jnp.broadcast_to(part, (8, 128))
    start_sum(0, "span", me, sum1)
    loop(MIDDLE, CHUNKS, send_rows)

    def wait_chunk(j):
        pltpu.make_async_copy(rhs.at[pl.ds(0, 3)], rhs.at[pl.ds(0, 3)], recv2.at[j]).wait()

    wait_chunk(0)
    loop(0, S // C, sweep1)

    halos(q1, hs1, hr1)

    def chunk(j):
        wait_chunk(j)
        before, now = done_after(j - 1), done_after(j)
        loop(before, now, sweep1)
        loop(jnp.where(j == 1, 0, before - 2), jnp.where(j == CHUNKS - 1, X, now - 2), sweep2)

    loop(1, 6, chunk)
    sum2[st] = end_sum(0, sum1)
    start_sum(1, "stream", st, sum2)
    loop(6, 8, chunk)
    total = end_sum(1, sum2)
    scale = 1.0 / math.sqrt(256 * 128)
    group = lax.div(lax.broadcasted_iota(jnp.int32, (1, 128), 1), X)
    for m in range(2):
        for r in range(2):
            forces[m, r] = jnp.sum(jnp.where(group == 2 * m + r, total[0:1], 0.0)) * scale

    loop(8, CHUNKS, chunk)

    for phase, buf in enumerate((sum1, sum2)):
        arrived(buf.at[pl.ds(0, 15)], ps.at[phase])
    arrived(wsend.at[pl.ds(0, S - 1)], ws)
    arrived(fv.at[pl.ds(0, S - 1)], fs.at[0])
    arrived(mv.at[pl.ds(0, S - 1)], fs.at[1])
    arrived(fbuf.at[:, pl.ds(0, NZ - Z), :], send1)
    arrived(sbuf.at[:, pl.ds(0, NZ - Z), :], send2)

    @pl.when(inner_l)
    def _():
        arrived(q0.at[0], hs0.at[0])
        arrived(q1.at[0], hs1.at[0])
        arrived(q1.at[0], hs2.at[0])

    @pl.when(inner_r)
    def _():
        arrived(q0.at[0], hs0.at[1])
        arrived(q1.at[0], hs1.at[1])
        arrived(q1.at[0], hs2.at[1])

    arrived(q2, osem)


def shards(forcing, initial_state, diagonal, span_speed, coupling, stiffener_mask, face_index, mode_shapes):
    high, low = table_rows()
    anyw = pl.BlockSpec(memory_space=pl.ANY)
    smem = pl.BlockSpec(memory_space=pltpu.SMEM)
    vm = pltpu.VMEM
    dma = pltpu.SemaphoreType.DMA
    flow, forces = pl.pallas_call(
        kernel,
        out_shape=(
            pltpu.VMEM((K, C, 2, X, 1, Y), f32),
            jax.ShapeDtypeStruct((2, 2), f32),
        ),
        in_specs=[anyw, anyw, anyw, smem, smem, anyw, anyw, anyw, anyw, anyw],
        out_specs=(pl.BlockSpec(memory_space=pltpu.VMEM), smem),
        scratch_shapes=[
            vm((NZ, NZ), bf16), vm((NZ, NZ), bf16),
            vm((CHUNKS, NZ, Y), f32), vm((CHUNKS, NZ, Y), f32),
            vm((X, C, KR, Y), f32),
            vm((X + 2, C, KR, Y), f32), vm((X + 2, C, KR, Y), f32), vm((X, C, KR, Y), f32),
            vm((X, C, KR, Y), f32),
            vm((X, C, K, Y), f32), vm((X, C, K, Y), f32),
            vm((100, 8, Y), f32),
            vm((C, X, Y), f32), vm((X, Y), jnp.int32), vm((C, K, Y), f32),
            vm((S, 2, 128), jnp.int32), vm((S, 2, 2, 128), f32),
            vm((NZ, 128), f32), vm((KR, 128), f32), vm((KR, 128), f32),
            vm((16, 8, 128), f32), vm((16, 8, 128), f32),
            vm((2, 128), jnp.int32), vm((2, 2, 128), f32),
            vm((S, 8, Y), f32), vm((S, 8, Y), f32), vm((X, C, KR, Y), f32), vm((X + 2, C, KR, Y), f32),
            dma((2,)), dma, dma((2,)), dma((2,)),
            dma, dma((CHUNKS,)), dma, dma((CHUNKS,)),
            dma((2,)), dma((2,)), dma((2,)), dma((2,)), dma((2,)), dma((2,)), dma, dma,
            dma((2,)), dma((2,)), dma((2,)), dma((2,)), dma,
        ],
        compiler_params=pltpu.CompilerParams(
            collective_id=0, has_side_effects=True, vmem_limit_bytes=64_350_000
        ),
    )(
        forcing.reshape(C, Z, X, 1, Y),
        initial_state.reshape(K, C, 2, X, 1, Y),
        diagonal, span_speed, coupling.transpose(1, 0, 2), stiffener_mask, face_index, mode_shapes,
        jnp.asarray(high), jnp.asarray(low),
    )
    return flow.reshape(K, C, 2, X, Y), forces


def solution(mesh):
    return jax.shard_map(
        shards,
        mesh=mesh,
        in_specs=(
            P(None, "span", "stream", None),
            P("span", None, None, "stream", None),
            P(),
            P(),
            P(),
            P(),
            P(None, ("stream", "span")),
            P(None, None, ("stream", "span")),
        ),
        out_specs=(P("span", None, None, "stream", None), P()),
        check_vma=False,
    )
```

```python
import functools
import math

import jax
import jax.numpy as jnp
import numpy as np
from jax import lax
from jax.experimental import pallas as pl
from jax.experimental.pallas import tpu as pltpu
from jax.sharding import PartitionSpec as P

MESH = pl.DeviceIdType.MESH
S = 16
N = 16
K = 16
C = 5
X = 32
Z = 32
Y = 128
NZ = 512
KR = 2 * K
CHUNKS = X * C // S
HELD = 8
EARLY = 1
MIDDLE = 8
f32 = jnp.float32
bf16 = jnp.bfloat16


def table_rows():
    z = np.arange(NZ)
    k = np.arange(NZ // 2)
    phase = (k[:, None] * z[None, :] % NZ) * (2.0 * math.pi / NZ)
    both = np.stack([np.cos(phase), -np.sin(phase)], 0) / math.sqrt(NZ)
    rows = both.reshape(2, S, 2, 8, NZ).transpose(1, 2, 0, 3, 4).reshape(NZ, NZ)
    exact = rows.astype(np.float32)
    high = exact.astype(jnp.bfloat16)
    low = (exact - high.astype(np.float32)).astype(jnp.bfloat16)
    return high, low


def split(v):
    high = v.astype(bf16)
    return high, (v - high.astype(f32)).astype(bf16)


def dot3(ah, al, bh, bl):
    d = functools.partial(jnp.dot, preferred_element_type=f32)
    return d(ah, bh) + (d(ah, bl) + d(al, bh))


def cell(order):
    half = lax.div(order, 2)
    return jnp.where(lax.rem(order, 2) == 0, half, X - 1 - half)


def row_of(j, p):
    rho = j * S + p
    return cell(lax.div(rho, C)), lax.rem(rho, C)


def done_after(j):
    return lax.div((j + 1) * S, C)


def far_first(i):
    half = lax.div(i + 1, 2)
    return jnp.where(lax.rem(i, 2) == 1, S // 2 - half, S // 2 + half)


def loop(lo, hi, body):
    def step(i, carry):
        body(i)
        return carry

    lax.fori_loop(lo, hi, step, 0)


def kernel(
    forcing, init, diag, speed, coup, mask, faces, modes, thigh, tlow,
    flow, forces,
    th, tl, fbuf, sbuf, rhs, q0, q1, near0, alpha, beta, coef, dv, kv, bv,
    fv, mv, wallm, gv, wall, sum1, sum2, fown, mown,
    wsend, wrecv, rhsw, q1w,
    sem_t, sem_q, sem_d, sem_f, send1, recv1, send2, recv2,
    hs0, hr0, hs1, hr1, hs2, hr2, ws, wr, fs, fr, ps, pr,
):
    me = lax.axis_index("span")
    st = lax.axis_index("stream")
    first, last = st == 0, st == N - 1
    inner_l, inner_r = st > 0, st < N - 1

    def remote(src, dst, ss, rs, axis, to):
        return pltpu.make_async_remote_copy(
            src_ref=src, dst_ref=dst, send_sem=ss, recv_sem=rs, device_id={axis: to}, device_id_type=MESH
        )

    def arrived(ref, sem):
        pltpu.make_async_copy(ref, ref, sem).wait()

    barrier = pltpu.get_barrier_semaphore()

    def greet(i):
        pl.semaphore_signal(barrier, inc=1, device_id={"span": lax.rem(me + i, S)}, device_id_type=MESH)
        pl.semaphore_signal(barrier, inc=1, device_id={"stream": lax.rem(st + i, N)}, device_id_type=MESH)

    loop(1, S, greet)

    x0 = pl.multiple_of(st * X, X)
    cp_d = pltpu.make_async_copy(diag.at[:, pl.ds(x0, X), :], dv, sem_d.at[0])
    cp_k = pltpu.make_async_copy(mask.at[pl.ds(x0, X), :], kv, sem_d.at[1])
    cp_d.start()
    cp_k.start()
    cp_h = pltpu.make_async_copy(thigh, th, sem_t.at[0])
    cp_l = pltpu.make_async_copy(tlow, tl, sem_t.at[1])
    cp_h.start()
    cp_l.start()
    cp_f = pltpu.make_async_copy(faces, fown, sem_f.at[0])
    cp_m = pltpu.make_async_copy(modes, mown, sem_f.at[1])
    cp_f.start()
    cp_m.start()

    mine = pl.multiple_of(me * Z, Z)

    def own_rows(j):
        x, c = row_of(j, me)
        pltpu.make_async_copy(forcing.at[c, :, x, 0, :], fbuf.at[j, pl.ds(mine, Z), :], recv1.at[j]).start()

    loop(0, CHUNKS, own_rows)

    def load_state(x):
        for c in range(C):
            for r in range(2):
                for h in range(2):
                    pltpu.make_async_copy(
                        init.at[pl.ds(8 * h, 8), c, r, x, 0, :], q0.at[x + 1, c, pl.ds(K * h + 8 * r, 8), :], sem_q
                    ).start()

    loop(0, X, load_state)

    for a in range(4):
        for c in range(C):
            for d in range(C):
                coef[a * 25 + c * 5 + d] = jnp.full((8, Y), coup[c, a, d], f32)
    k_index = (me * K + lax.broadcasted_iota(jnp.int32, (K, Y), 0)).astype(f32)
    for c in range(C):
        bv[c] = k_index * (2.0 * math.pi / NZ) * speed[c]

    @pl.when(first)
    def _():
        q0[0] = jnp.zeros((C, KR, Y), f32)
        q1[0] = jnp.zeros((C, KR, Y), f32)
        q1w[0] = jnp.zeros((C, KR, Y), f32)

    @pl.when(last)
    def _():
        q0[X + 1] = jnp.zeros((C, KR, Y), f32)
        q1[X + 1] = jnp.zeros((C, KR, Y), f32)
        q1w[X + 1] = jnp.zeros((C, KR, Y), f32)

    cp_f.wait()
    cp_m.wait()
    core = lax.rem(me, 2)
    sibling = me + 1 - 2 * core
    slot = core * (S // 2) + lax.div(me, 2)
    fv[slot] = fown[...]
    mv[slot] = mown[...]
    pl.semaphore_wait(barrier, 2 * S - 2)

    def halo0(c):
        for r in range(2):
            for h in range(2):
                rows, ks = pl.ds(K * h + 8 * r, 8), pl.ds(8 * h, 8)

                @pl.when(inner_l)
                def _():
                    remote(init.at[ks, c, r, 0, 0, :], q0.at[X + 1, c, rows, :], hs0.at[0], hr0.at[1], "stream", st - 1).start()

                @pl.when(inner_r)
                def _():
                    remote(init.at[ks, c, r, X - 1, 0, :], q0.at[0, c, rows, :], hs0.at[1], hr0.at[0], "stream", st + 1).start()

    loop(0, C, halo0)

    def send_forcing(j):
        def one(i):
            t = lax.rem(me + i, S)
            x, c = row_of(j, t)
            remote(
                forcing.at[c, :, x, 0, :], fbuf.at[j, pl.ds(mine, Z), :], send1, recv1.at[j], "span", t
            ).start()

        loop(1, S, one)

    def send_faces(i):
        t = lax.rem(me + 2 * i, S)
        remote(fown, fv.at[slot], fs.at[0], fr.at[0], "span", t).start()
        remote(mown, mv.at[slot], fs.at[1], fr.at[1], "span", t).start()

    send_forcing(0)
    loop(1, S // 2, send_faces)
    loop(1, CHUNKS, send_forcing)

    cp_d.wait()
    cp_k.wait()

    def factors(x):
        keep = 1.0 - kv[pl.ds(x, 1), :].astype(f32)
        for c in range(C):
            a = jnp.broadcast_to(dv[c, pl.ds(x, 1), :], (K, Y))
            b = bv[c]
            scale = keep / (a * a + b * b)
            alpha[x, c] = a * scale
            beta[x, c] = b * scale

    loop(0, X, factors)

    lane = lax.broadcasted_iota(jnp.int32, (KR, Y), 1)

    def near(q, x, outs=tuple(range(C)), rows=pl.ds(0, KR)):
        acc = [None] * len(outs)
        for d in range(C):
            here = q[x + 1, d, rows]
            up = jnp.where(lane[: rows.size] < Y - 1, pltpu.roll(here, Y - 1, 1), 0.0)
            down = jnp.where(lane[: rows.size] > 0, pltpu.roll(here, 1, 1), 0.0)
            for a, v in enumerate((q[x + 2, d, rows], q[x, d, rows], up, down)):
                v = v.reshape(rows.size // 8, 8, Y)
                for i, c in enumerate(outs):
                    term = coef[a * 25 + c * 5 + d][None] * v
                    acc[i] = term if acc[i] is None else acc[i] + term
        return [v.reshape(rows.size, Y) for v in acc]

    arrived(q0.at[pl.ds(1, X)], sem_q)

    @pl.when(inner_l)
    def _():
        arrived(q0.at[0], hr0.at[0])

    @pl.when(inner_r)
    def _():
        arrived(q0.at[X + 1], hr0.at[1])

    def first_near(x):
        for c, v in enumerate(near(q0, x)):
            near0[x, c] = v

    loop(0, X, first_near)

    cp_h.wait()
    cp_l.wait()

    def transform(j):
        arrived(fbuf.at[j], recv1.at[j])
        fh, fl = split(fbuf[j])
        for i in range(4):
            part = pl.ds(i * 128, 128)
            value = dot3(th[part, :], tl[part, :], fh, fl)
            sbuf[j, part, :] = value
            value = value.reshape(4, 4, 8, Y)
            for g in range(4):
                moved = pltpu.roll(value[:, g].reshape(KR, Y), X * g + 2 * j, 1)
                kept = jnp.where(lax.div(lane, 2) == 16 * g + j, moved, 0.0)
                wsend[pl.ds(4 * i, 4)] += kept.reshape(4, 8, Y)
        x, c = row_of(j, me)
        rhs[x, c] = sbuf[j, pl.ds(mine, KR), :]

    def send_half(h):
        x, c = row_of(CHUNKS - 1, me)
        rows = pl.ds(K * h, K)

        def one(i):
            t = lax.rem(me + far_first(i), S)
            rows_t = pl.ds(pl.multiple_of(t * KR + K * h, K), K)
            remote(
                sbuf.at[CHUNKS - 1, rows_t, :], rhs.at[x, c, rows, :], send2, recv2.at[CHUNKS - 1 + h], "span", t
            ).start()

        loop(0, S - 1, one)

    def send_rows(j):
        x, c = row_of(j, me)

        def one(i):
            t = lax.rem(me + far_first(i), S)
            rows_t = pl.ds(pl.multiple_of(t * KR, KR), KR)
            remote(sbuf.at[j, rows_t, :], rhs.at[x, c], send2, recv2.at[j], "span", t).start()

        loop(0, S - 1, one)

    wsend[...] = jnp.zeros((S, 8, Y), f32)
    loop(0, HELD, transform)
    loop(0, EARLY, send_rows)
    others, same = pl.ds(0, S // 2 - 1), pl.ds(pl.multiple_of(core * (S // 2), S // 2), S // 2)
    for i, ref in enumerate((fv, mv)):
        arrived(ref.at[others], fr.at[i])
        remote(ref.at[same], ref.at[same], fs.at[2 + i], fr.at[2 + i], "span", sibling).start()
    loop(HELD, CHUNKS, transform)
    wrecv[me] = wsend[me]

    def send_wall(i):
        t = lax.rem(me + i, S)
        remote(wsend.at[t], wrecv.at[me], ws, wr, "span", t).start()

    loop(1, S, send_wall)
    loop(EARLY, MIDDLE, send_rows)

    arrived(fv.at[same], fr.at[2])
    arrived(mv.at[same], fr.at[3])
    z_row = lax.broadcasted_iota(jnp.int32, (Z, 128), 0)
    x_row = lax.broadcasted_iota(jnp.int32, (128, 128), 0)

    def scatter(s):
        total = jnp.zeros((Z, 128), f32)
        for m in range(2):
            index = fv[s, pl.ds(m, 1), :]
            at_z = z_row == lax.div(index, X)
            for r in range(2):
                placed = (x_row == lax.rem(index, X) + (2 * m + r) * X).astype(f32)
                value = jnp.where(at_z, mv[s, m, pl.ds(r, 1), :], 0.0)
                total = total + lax.dot_general(
                    value, placed, (((1,), (1,)), ((), ())),
                    precision=lax.Precision.HIGHEST, preferred_element_type=f32,
                )
        place = 2 * lax.rem(s, S // 2) + lax.div(s, S // 2)
        wallm[pl.ds(pl.multiple_of(place * Z, Z), Z), :] = total

    loop(0, S, scatter)
    wh, wl = split(wallm[...])
    own_k = pl.ds(pl.multiple_of(me * KR, KR), KR)
    row = lax.broadcasted_iota(jnp.int32, (KR, Y), 0)
    zero_k = jnp.logical_and(me == 0, jnp.logical_and(row < K, lax.rem(row, 8) == 0))
    weight = jnp.where(zero_k, 1.0, 2.0)
    gv[...] = weight * dot3(th[own_k, :], tl[own_k, :], wh, wl)
    wall[...] = jnp.zeros((KR, 128), f32)

    def invert(x, c, d, ks=pl.ds(0, K)):
        d = d.reshape(ks.size // 8, 2, 8, Y)
        re, im = d[:, 0], d[:, 1]
        al = alpha[x, c, ks].reshape(ks.size // 8, 8, Y)
        be = beta[x, c, ks].reshape(ks.size // 8, 8, Y)
        return al * re + be * im, al * im - be * re

    def both(re, im):
        return jnp.stack([re, im], 1).reshape(-1, Y)

    whole = (pl.ds(0, KR), pl.ds(0, K))

    def sweep1(order, part=whole):
        rows, ks = part
        x = cell(order)
        for c in range(C):
            q1[x + 1, c, rows] = both(*invert(x, c, rhs[x, c, rows] - near0[x, c, rows], ks))

    def sweep2(order, part=whole):
        rows, ks = part
        x = cell(order)
        for c, v in enumerate(near(q1, x, rows=rows)):
            for r, u in enumerate(invert(x, c, rhs[x, c, rows] - v, ks)):
                at = (ks.start * C * 2 + 2 * c + r) * X + x
                flow[pl.ds(at, ks.size, stride=2 * C * X), :] = u.reshape(ks.size, Y)

    def halos(q, hs, hr):
        @pl.when(inner_l)
        def _():
            remote(q.at[1], q.at[X + 1], hs.at[0], hr.at[1], "stream", st - 1).start()

        @pl.when(inner_r)
        def _():
            remote(q.at[X], q.at[0], hs.at[1], hr.at[0], "stream", st + 1).start()

        @pl.when(inner_l)
        def _():
            arrived(q.at[0], hr.at[0])

        @pl.when(inner_r)
        def _():
            arrived(q.at[X + 1], hr.at[1])

    arrived(wrecv.at[pl.ds(0, S - 1)], wr)

    def unpack(p):
        tile = wrecv[p]
        for j in range(CHUNKS):
            x, c = row_of(j, p)
            for g in range(4):
                rhsw[x, c, 8 * g : 8 * g + 8] = pltpu.roll(tile, (Y - X * g - 2 * j) % Y, 1)
            q1w[x + 1, c] = both(*invert(x, c, rhsw[x, c] - near0[x, c]))

    loop(0, S, unpack)
    halos(q1w, hs2, hr2)

    def wall_values(x):
        (v,) = near(q1w, x, (C - 1,))
        at = both(*invert(x, C - 1, rhsw[x, C - 1] - v))[:, 0:1]
        wall[...] += jnp.where(lax.rem(lane, X) == x, at, 0.0)

    loop(0, X, wall_values)
    part = jnp.sum(wall[...] * gv[...], axis=0, keepdims=True)

    def start_sum(phase, axis, pos, buf):
        def one(i):
            remote(buf.at[pos], buf.at[pos], ps.at[phase], pr.at[phase], axis, lax.rem(pos + i, 16)).start()

        loop(1, 16, one)

    def end_sum(phase, buf):
        arrived(buf.at[pl.ds(0, 15)], pr.at[phase])
        total = buf[0]
        for i in range(1, 16):
            total = total + buf[i]
        return total

    sum1[me] = jnp.broadcast_to(part, (8, 128))
    start_sum(0, "span", me, sum1)
    loop(MIDDLE, CHUNKS - 1, send_rows)
    send_half(0)
    send_half(1)

    def wait_chunk(j):
        pltpu.make_async_copy(rhs.at[pl.ds(0, 3)], rhs.at[pl.ds(0, 3)], recv2.at[j]).wait()

    wait_chunk(0)
    loop(0, S // C, sweep1)

    halos(q1, hs1, hr1)

    def chunk(j):
        wait_chunk(j)
        before, now = done_after(j - 1), done_after(j)
        loop(before, now, sweep1)
        loop(jnp.where(j == 1, 0, before - 2), now - 2, sweep2)

    loop(1, 6, chunk)
    sum2[st] = end_sum(0, sum1)
    start_sum(1, "stream", st, sum2)
    loop(6, 8, chunk)
    total = end_sum(1, sum2)
    scale = 1.0 / math.sqrt(256 * 128)
    group = lax.div(lax.broadcasted_iota(jnp.int32, (1, 128), 1), X)
    for m in range(2):
        for r in range(2):
            forces[m, r] = jnp.sum(jnp.where(group == 2 * m + r, total[0:1], 0.0)) * scale

    loop(8, CHUNKS - 1, chunk)
    for h in range(2):
        part = (pl.ds(K * h, K), pl.ds(8 * h, 8))
        pltpu.make_async_copy(
            rhs.at[pl.ds(0, 3), :, pl.ds(0, K), :], rhs.at[pl.ds(0, 3), :, pl.ds(0, K), :], recv2.at[CHUNKS - 1 + h]
        ).wait()
        known = (CHUNKS - 1) * S // C
        loop(known, X, lambda order: sweep1(order, part))
        loop(known - 2, X, lambda order: sweep2(order, part))

    for phase, buf in enumerate((sum1, sum2)):
        arrived(buf.at[pl.ds(0, 15)], ps.at[phase])
    arrived(wsend.at[pl.ds(0, S - 1)], ws)
    arrived(fv.at[others], fs.at[0])
    arrived(mv.at[others], fs.at[1])
    arrived(fv.at[same], fs.at[2])
    arrived(mv.at[same], fs.at[3])
    arrived(fbuf.at[:, pl.ds(0, NZ - Z), :], send1)
    arrived(sbuf.at[:, pl.ds(0, NZ - Z), :], send2)

    @pl.when(inner_l)
    def _():
        arrived(q0.at[0], hs0.at[0])
        arrived(q1.at[0], hs1.at[0])
        arrived(q1.at[0], hs2.at[0])

    @pl.when(inner_r)
    def _():
        arrived(q0.at[0], hs0.at[1])
        arrived(q1.at[0], hs1.at[1])
        arrived(q1.at[0], hs2.at[1])


def shards(forcing, initial_state, diagonal, span_speed, coupling, stiffener_mask, face_index, mode_shapes):
    high, low = table_rows()
    anyw = pl.BlockSpec(memory_space=pl.ANY)
    smem = pl.BlockSpec(memory_space=pltpu.SMEM)
    vm = pltpu.VMEM
    dma = pltpu.SemaphoreType.DMA
    flow, forces = pl.pallas_call(
        kernel,
        out_shape=(
            pltpu.VMEM((K * C * 2 * X, Y), f32),
            jax.ShapeDtypeStruct((2, 2), f32),
        ),
        in_specs=[anyw, anyw, anyw, smem, smem, anyw, anyw, anyw, anyw, anyw],
        out_specs=(pl.BlockSpec(memory_space=pltpu.VMEM), smem),
        scratch_shapes=[
            vm((NZ, NZ), bf16), vm((NZ, NZ), bf16),
            vm((CHUNKS, NZ, Y), f32), vm((CHUNKS, NZ, Y), f32),
            vm((X, C, KR, Y), f32),
            vm((X + 2, C, KR, Y), f32), vm((X + 2, C, KR, Y), f32), vm((X, C, KR, Y), f32),
            vm((X, C, K, Y), f32), vm((X, C, K, Y), f32),
            vm((100, 8, Y), f32),
            vm((C, X, Y), f32), vm((X, Y), jnp.int32), vm((C, K, Y), f32),
            vm((S, 2, 128), jnp.int32), vm((S, 2, 2, 128), f32),
            vm((NZ, 128), f32), vm((KR, 128), f32), vm((KR, 128), f32),
            vm((16, 8, 128), f32), vm((16, 8, 128), f32),
            vm((2, 128), jnp.int32), vm((2, 2, 128), f32),
            vm((S, 8, Y), f32), vm((S, 8, Y), f32), vm((X, C, KR, Y), f32), vm((X + 2, C, KR, Y), f32),
            dma((2,)), dma, dma((2,)), dma((2,)),
            dma, dma((CHUNKS,)), dma, dma((CHUNKS + 1,)),
            dma((2,)), dma((2,)), dma((2,)), dma((2,)), dma((2,)), dma((2,)), dma, dma,
            dma((4,)), dma((4,)), dma((2,)), dma((2,)),
        ],
        compiler_params=pltpu.CompilerParams(
            collective_id=0, has_side_effects=True, vmem_limit_bytes=64_350_000
        ),
    )(
        forcing.reshape(C, Z, X, 1, Y),
        initial_state.reshape(K, C, 2, X, 1, Y),
        diagonal, span_speed, coupling.transpose(1, 0, 2), stiffener_mask, face_index, mode_shapes,
        jnp.asarray(high), jnp.asarray(low),
    )
    return flow.reshape(K, C, 2, X, Y), forces


def solution(mesh):
    return jax.shard_map(
        shards,
        mesh=mesh,
        in_specs=(
            P(None, "span", "stream", None),
            P("span", None, None, "stream", None),
            P(),
            P(),
            P(),
            P(),
            P(None, ("stream", "span")),
            P(None, None, ("stream", "span")),
        ),
        out_specs=(P("span", None, None, "stream", None), P()),
        check_vma=False,
    )
```

```python
import functools
import math

import jax
import jax.numpy as jnp
import numpy as np
from jax import lax
from jax.experimental import pallas as pl
from jax.experimental.pallas import tpu as pltpu
from jax.sharding import PartitionSpec as P

MESH = pl.DeviceIdType.MESH
S = 16
N = 16
K = 16
C = 5
X = 32
Z = 32
Y = 128
NZ = 512
KR = 2 * K
CHUNKS = X * C // S
HELD = 8
EARLY = 1
MIDDLE = 7
f32 = jnp.float32
bf16 = jnp.bfloat16


def table_rows():
    z = np.arange(NZ)
    k = np.arange(NZ // 2)
    phase = (k[:, None] * z[None, :] % NZ) * (2.0 * math.pi / NZ)
    both = np.stack([np.cos(phase), -np.sin(phase)], 0) / math.sqrt(NZ)
    rows = both.reshape(2, S, 2, 8, NZ).transpose(1, 2, 0, 3, 4).reshape(NZ, NZ)
    exact = rows.astype(np.float32)
    high = exact.astype(jnp.bfloat16)
    low = (exact - high.astype(np.float32)).astype(jnp.bfloat16)
    return high, low


def split(v):
    high = v.astype(bf16)
    return high, (v - high.astype(f32)).astype(bf16)


def dot3(ah, al, bh, bl):
    d = functools.partial(jnp.dot, preferred_element_type=f32)
    return d(ah, bh) + (d(ah, bl) + d(al, bh))


def cell(order):
    half = lax.div(order, 2)
    return jnp.where(lax.rem(order, 2) == 0, half, X - 1 - half)


def row_of(j, p):
    rho = j * S + p
    return cell(lax.div(rho, C)), lax.rem(rho, C)


def done_after(j):
    return lax.div((j + 1) * S, C)


def far_first(i):
    half = lax.div(i + 1, 2)
    return jnp.where(lax.rem(i, 2) == 1, S // 2 - half, S // 2 + half)


def loop(lo, hi, body):
    def step(i, carry):
        body(i)
        return carry

    lax.fori_loop(lo, hi, step, 0)


def kernel(
    forcing, init, diag, speed, coup, mask, faces, modes, thigh, tlow,
    flow, forces,
    th, tl, fbuf, sbuf, rhs, q0, q1, near0, alpha, beta, coef, dv, kv, bv,
    fv, mv, wallm, gv, wall, sum1, sum2, fown, mown,
    wsend, wrecv, rhsw, q1w,
    sem_t, sem_q, sem_d, sem_f, send1, recv1, send2, recv2,
    hs0, hr0, hs1, hr1, hs2, hr2, ws, wr, fs, fr, ps, pr,
):
    me = lax.axis_index("span")
    st = lax.axis_index("stream")
    first, last = st == 0, st == N - 1
    inner_l, inner_r = st > 0, st < N - 1

    def remote(src, dst, ss, rs, axis, to):
        return pltpu.make_async_remote_copy(
            src_ref=src, dst_ref=dst, send_sem=ss, recv_sem=rs, device_id={axis: to}, device_id_type=MESH
        )

    def arrived(ref, sem):
        pltpu.make_async_copy(ref, ref, sem).wait()

    barrier = pltpu.get_barrier_semaphore()

    def greet(i):
        pl.semaphore_signal(barrier, inc=1, device_id={"span": lax.rem(me + i, S)}, device_id_type=MESH)
        pl.semaphore_signal(barrier, inc=1, device_id={"stream": lax.rem(st + i, N)}, device_id_type=MESH)

    loop(1, S, greet)

    x0 = pl.multiple_of(st * X, X)
    cp_d = pltpu.make_async_copy(diag.at[:, pl.ds(x0, X), :], dv, sem_d.at[0])
    cp_k = pltpu.make_async_copy(mask.at[pl.ds(x0, X), :], kv, sem_d.at[1])
    cp_d.start()
    cp_k.start()
    cp_h = pltpu.make_async_copy(thigh, th, sem_t.at[0])
    cp_l = pltpu.make_async_copy(tlow, tl, sem_t.at[1])
    cp_h.start()
    cp_l.start()
    cp_f = pltpu.make_async_copy(faces, fown, sem_f.at[0])
    cp_m = pltpu.make_async_copy(modes, mown, sem_f.at[1])
    cp_f.start()
    cp_m.start()

    mine = pl.multiple_of(me * Z, Z)

    def own_rows(j):
        x, c = row_of(j, me)
        pltpu.make_async_copy(forcing.at[c, :, x, 0, :], fbuf.at[j, pl.ds(mine, Z), :], recv1.at[j]).start()

    loop(0, CHUNKS, own_rows)

    def load_state(x):
        for c in range(C):
            for r in range(2):
                for h in range(2):
                    pltpu.make_async_copy(
                        init.at[pl.ds(8 * h, 8), c, r, x, 0, :], q0.at[x + 1, c, pl.ds(K * h + 8 * r, 8), :], sem_q
                    ).start()

    loop(0, X, load_state)

    for a in range(4):
        for c in range(C):
            for d in range(C):
                coef[a * 25 + c * 5 + d] = jnp.full((8, Y), coup[c, a, d], f32)
    k_index = (me * K + lax.broadcasted_iota(jnp.int32, (K, Y), 0)).astype(f32)
    for c in range(C):
        bv[c] = k_index * (2.0 * math.pi / NZ) * speed[c]

    @pl.when(first)
    def _():
        q0[0] = jnp.zeros((C, KR, Y), f32)
        q1[0] = jnp.zeros((C, KR, Y), f32)
        q1w[0] = jnp.zeros((C, KR, Y), f32)

    @pl.when(last)
    def _():
        q0[X + 1] = jnp.zeros((C, KR, Y), f32)
        q1[X + 1] = jnp.zeros((C, KR, Y), f32)
        q1w[X + 1] = jnp.zeros((C, KR, Y), f32)

    cp_f.wait()
    cp_m.wait()
    core = lax.rem(me, 2)
    sibling = me + 1 - 2 * core
    slot = core * (S // 2) + lax.div(me, 2)
    fv[slot] = fown[...]
    mv[slot] = mown[...]
    pl.semaphore_wait(barrier, 2 * S - 2)

    def halo0(c):
        for r in range(2):
            for h in range(2):
                rows, ks = pl.ds(K * h + 8 * r, 8), pl.ds(8 * h, 8)

                @pl.when(inner_l)
                def _():
                    remote(init.at[ks, c, r, 0, 0, :], q0.at[X + 1, c, rows, :], hs0.at[0], hr0.at[1], "stream", st - 1).start()

                @pl.when(inner_r)
                def _():
                    remote(init.at[ks, c, r, X - 1, 0, :], q0.at[0, c, rows, :], hs0.at[1], hr0.at[0], "stream", st + 1).start()

    loop(0, C, halo0)

    def send_forcing(j):
        def one(i):
            t = lax.rem(me + far_first(i), S)
            x, c = row_of(j, t)
            remote(
                forcing.at[c, :, x, 0, :], fbuf.at[j, pl.ds(mine, Z), :], send1, recv1.at[j], "span", t
            ).start()

        loop(0, S - 1, one)

    def send_faces(i):
        t = lax.rem(me + 2 * i, S)
        remote(fown, fv.at[slot], fs.at[0], fr.at[0], "span", t).start()
        remote(mown, mv.at[slot], fs.at[1], fr.at[1], "span", t).start()

    send_forcing(0)
    loop(1, S // 2, send_faces)
    loop(1, CHUNKS, send_forcing)

    cp_d.wait()
    cp_k.wait()

    def factors(x):
        keep = 1.0 - kv[pl.ds(x, 1), :].astype(f32)
        for c in range(C):
            a = jnp.broadcast_to(dv[c, pl.ds(x, 1), :], (K, Y))
            b = bv[c]
            scale = keep / (a * a + b * b)
            alpha[x, c] = a * scale
            beta[x, c] = b * scale

    loop(0, X, factors)

    lane = lax.broadcasted_iota(jnp.int32, (KR, Y), 1)

    def near(q, x, outs=tuple(range(C)), rows=pl.ds(0, KR)):
        acc = [None] * len(outs)
        for d in range(C):
            here = q[x + 1, d, rows]
            up = jnp.where(lane[: rows.size] < Y - 1, pltpu.roll(here, Y - 1, 1), 0.0)
            down = jnp.where(lane[: rows.size] > 0, pltpu.roll(here, 1, 1), 0.0)
            for a, v in enumerate((q[x + 2, d, rows], q[x, d, rows], up, down)):
                v = v.reshape(rows.size // 8, 8, Y)
                for i, c in enumerate(outs):
                    term = coef[a * 25 + c * 5 + d][None] * v
                    acc[i] = term if acc[i] is None else acc[i] + term
        return [v.reshape(rows.size, Y) for v in acc]

    arrived(q0.at[pl.ds(1, X)], sem_q)

    @pl.when(inner_l)
    def _():
        arrived(q0.at[0], hr0.at[0])

    @pl.when(inner_r)
    def _():
        arrived(q0.at[X + 1], hr0.at[1])

    def first_near(x):
        for c, v in enumerate(near(q0, x)):
            near0[x, c] = v

    loop(0, X, first_near)

    cp_h.wait()
    cp_l.wait()

    def transform(j):
        arrived(fbuf.at[j], recv1.at[j])
        fh, fl = split(fbuf[j])
        for i in range(4):
            part = pl.ds(i * 128, 128)
            value = dot3(th[part, :], tl[part, :], fh, fl)
            sbuf[j, part, :] = value
            value = value.reshape(4, 4, 8, Y)
            for g in range(4):
                moved = pltpu.roll(value[:, g].reshape(KR, Y), X * g + 2 * j, 1)
                kept = jnp.where(lax.div(lane, 2) == 16 * g + j, moved, 0.0)
                wsend[pl.ds(4 * i, 4)] += kept.reshape(4, 8, Y)
        x, c = row_of(j, me)
        rhs[x, c] = sbuf[j, pl.ds(mine, KR), :]

    def send_half(h):
        x, c = row_of(CHUNKS - 1, me)
        rows = pl.ds(K * h, K)

        def one(i):
            t = lax.rem(me + far_first(i), S)
            rows_t = pl.ds(pl.multiple_of(t * KR + K * h, K), K)
            remote(
                sbuf.at[CHUNKS - 1, rows_t, :], rhs.at[x, c, rows, :], send2, recv2.at[CHUNKS - 1 + h], "span", t
            ).start()

        loop(0, S - 1, one)

    def send_rows(j):
        x, c = row_of(j, me)

        def one(i):
            t = lax.rem(me + far_first(i), S)
            rows_t = pl.ds(pl.multiple_of(t * KR, KR), KR)
            remote(sbuf.at[j, rows_t, :], rhs.at[x, c], send2, recv2.at[j], "span", t).start()

        loop(0, S - 1, one)

    wsend[...] = jnp.zeros((S, 8, Y), f32)
    loop(0, HELD, transform)
    loop(0, EARLY, send_rows)
    others, same = pl.ds(0, S // 2 - 1), pl.ds(pl.multiple_of(core * (S // 2), S // 2), S // 2)
    for i, ref in enumerate((fv, mv)):
        arrived(ref.at[others], fr.at[i])
        remote(ref.at[same], ref.at[same], fs.at[2 + i], fr.at[2 + i], "span", sibling).start()
    loop(HELD, CHUNKS, transform)
    wrecv[me] = wsend[me]

    def send_wall(i):
        t = lax.rem(me + i, S)
        remote(wsend.at[t], wrecv.at[me], ws, wr, "span", t).start()

    loop(1, S, send_wall)
    loop(EARLY, MIDDLE, send_rows)

    arrived(fv.at[same], fr.at[2])
    arrived(mv.at[same], fr.at[3])
    z_row = lax.broadcasted_iota(jnp.int32, (Z, 128), 0)
    x_row = lax.broadcasted_iota(jnp.int32, (128, 128), 0)

    def scatter(s):
        total = jnp.zeros((Z, 128), f32)
        for m in range(2):
            index = fv[s, pl.ds(m, 1), :]
            at_z = z_row == lax.div(index, X)
            for r in range(2):
                placed = (x_row == lax.rem(index, X) + (2 * m + r) * X).astype(f32)
                value = jnp.where(at_z, mv[s, m, pl.ds(r, 1), :], 0.0)
                total = total + lax.dot_general(
                    value, placed, (((1,), (1,)), ((), ())),
                    precision=lax.Precision.HIGHEST, preferred_element_type=f32,
                )
        place = 2 * lax.rem(s, S // 2) + lax.div(s, S // 2)
        wallm[pl.ds(pl.multiple_of(place * Z, Z), Z), :] = total

    loop(0, S, scatter)
    wh, wl = split(wallm[...])
    own_k = pl.ds(pl.multiple_of(me * KR, KR), KR)
    row = lax.broadcasted_iota(jnp.int32, (KR, Y), 0)
    zero_k = jnp.logical_and(me == 0, jnp.logical_and(row < K, lax.rem(row, 8) == 0))
    weight = jnp.where(zero_k, 1.0, 2.0)
    gv[...] = weight * dot3(th[own_k, :], tl[own_k, :], wh, wl)
    wall[...] = jnp.zeros((KR, 128), f32)

    def invert(x, c, d, ks=pl.ds(0, K)):
        d = d.reshape(ks.size // 8, 2, 8, Y)
        re, im = d[:, 0], d[:, 1]
        al = alpha[x, c, ks].reshape(ks.size // 8, 8, Y)
        be = beta[x, c, ks].reshape(ks.size // 8, 8, Y)
        return al * re + be * im, al * im - be * re

    def both(re, im):
        return jnp.stack([re, im], 1).reshape(-1, Y)

    whole = (pl.ds(0, KR), pl.ds(0, K))

    def sweep1(order, part=whole):
        rows, ks = part
        x = cell(order)
        for c in range(C):
            q1[x + 1, c, rows] = both(*invert(x, c, rhs[x, c, rows] - near0[x, c, rows], ks))

    def sweep2(order, part=whole):
        rows, ks = part
        x = cell(order)
        for c, v in enumerate(near(q1, x, rows=rows)):
            for r, u in enumerate(invert(x, c, rhs[x, c, rows] - v, ks)):
                at = (ks.start * C * 2 + 2 * c + r) * X + x
                flow[pl.ds(at, ks.size, stride=2 * C * X), :] = u.reshape(ks.size, Y)

    def halos(q, hs, hr):
        @pl.when(inner_l)
        def _():
            remote(q.at[1], q.at[X + 1], hs.at[0], hr.at[1], "stream", st - 1).start()

        @pl.when(inner_r)
        def _():
            remote(q.at[X], q.at[0], hs.at[1], hr.at[0], "stream", st + 1).start()

        @pl.when(inner_l)
        def _():
            arrived(q.at[0], hr.at[0])

        @pl.when(inner_r)
        def _():
            arrived(q.at[X + 1], hr.at[1])

    arrived(wrecv.at[pl.ds(0, S - 1)], wr)

    def unpack(p):
        tile = wrecv[p]
        for j in range(CHUNKS):
            x, c = row_of(j, p)
            for g in range(4):
                rhsw[x, c, 8 * g : 8 * g + 8] = pltpu.roll(tile, (Y - X * g - 2 * j) % Y, 1)
            q1w[x + 1, c] = both(*invert(x, c, rhsw[x, c] - near0[x, c]))

    loop(0, S, unpack)
    halos(q1w, hs2, hr2)

    def wall_values(x):
        (v,) = near(q1w, x, (C - 1,))
        at = both(*invert(x, C - 1, rhsw[x, C - 1] - v))[:, 0:1]
        wall[...] += jnp.where(lax.rem(lane, X) == x, at, 0.0)

    loop(0, X, wall_values)
    part = jnp.sum(wall[...] * gv[...], axis=0, keepdims=True)

    def start_sum(phase, axis, pos, buf):
        def one(i):
            remote(buf.at[pos], buf.at[pos], ps.at[phase], pr.at[phase], axis, lax.rem(pos + i, 16)).start()

        loop(1, 16, one)

    def end_sum(phase, buf):
        arrived(buf.at[pl.ds(0, 15)], pr.at[phase])
        total = buf[0]
        for i in range(1, 16):
            total = total + buf[i]
        return total

    sum1[me] = jnp.broadcast_to(part, (8, 128))
    start_sum(0, "span", me, sum1)
    loop(MIDDLE, CHUNKS - 1, send_rows)
    send_half(0)
    send_half(1)

    def wait_chunk(j):
        pltpu.make_async_copy(rhs.at[pl.ds(0, 3)], rhs.at[pl.ds(0, 3)], recv2.at[j]).wait()

    wait_chunk(0)
    loop(0, S // C, sweep1)

    halos(q1, hs1, hr1)

    def chunk(j):
        wait_chunk(j)
        before, now = done_after(j - 1), done_after(j)
        loop(before, now, sweep1)
        loop(jnp.where(j == 1, 0, before - 2), now - 2, sweep2)

    loop(1, 6, chunk)
    sum2[st] = end_sum(0, sum1)
    start_sum(1, "stream", st, sum2)
    loop(6, 8, chunk)
    total = end_sum(1, sum2)
    scale = 1.0 / math.sqrt(256 * 128)
    group = lax.div(lax.broadcasted_iota(jnp.int32, (1, 128), 1), X)
    for m in range(2):
        for r in range(2):
            forces[m, r] = jnp.sum(jnp.where(group == 2 * m + r, total[0:1], 0.0)) * scale

    loop(8, CHUNKS - 1, chunk)
    for h in range(2):
        part = (pl.ds(K * h, K), pl.ds(8 * h, 8))
        pltpu.make_async_copy(
            rhs.at[pl.ds(0, 3), :, pl.ds(0, K), :], rhs.at[pl.ds(0, 3), :, pl.ds(0, K), :], recv2.at[CHUNKS - 1 + h]
        ).wait()
        known = (CHUNKS - 1) * S // C
        loop(known, X, lambda order: sweep1(order, part))
        loop(known - 2, X, lambda order: sweep2(order, part))

    for phase, buf in enumerate((sum1, sum2)):
        arrived(buf.at[pl.ds(0, 15)], ps.at[phase])
    arrived(wsend.at[pl.ds(0, S - 1)], ws)
    arrived(fv.at[others], fs.at[0])
    arrived(mv.at[others], fs.at[1])
    arrived(fv.at[same], fs.at[2])
    arrived(mv.at[same], fs.at[3])
    arrived(fbuf.at[:, pl.ds(0, NZ - Z), :], send1)
    arrived(sbuf.at[:, pl.ds(0, NZ - Z), :], send2)

    @pl.when(inner_l)
    def _():
        arrived(q0.at[0], hs0.at[0])
        arrived(q1.at[0], hs1.at[0])
        arrived(q1.at[0], hs2.at[0])

    @pl.when(inner_r)
    def _():
        arrived(q0.at[0], hs0.at[1])
        arrived(q1.at[0], hs1.at[1])
        arrived(q1.at[0], hs2.at[1])


def shards(forcing, initial_state, diagonal, span_speed, coupling, stiffener_mask, face_index, mode_shapes):
    high, low = table_rows()
    anyw = pl.BlockSpec(memory_space=pl.ANY)
    smem = pl.BlockSpec(memory_space=pltpu.SMEM)
    vm = pltpu.VMEM
    dma = pltpu.SemaphoreType.DMA
    flow, forces = pl.pallas_call(
        kernel,
        out_shape=(
            pltpu.VMEM((K * C * 2 * X, Y), f32),
            jax.ShapeDtypeStruct((2, 2), f32),
        ),
        in_specs=[anyw, anyw, anyw, smem, smem, anyw, anyw, anyw, anyw, anyw],
        out_specs=(pl.BlockSpec(memory_space=pltpu.VMEM), smem),
        scratch_shapes=[
            vm((NZ, NZ), bf16), vm((NZ, NZ), bf16),
            vm((CHUNKS, NZ, Y), f32), vm((CHUNKS, NZ, Y), f32),
            vm((X, C, KR, Y), f32),
            vm((X + 2, C, KR, Y), f32), vm((X + 2, C, KR, Y), f32), vm((X, C, KR, Y), f32),
            vm((X, C, K, Y), f32), vm((X, C, K, Y), f32),
            vm((100, 8, Y), f32),
            vm((C, X, Y), f32), vm((X, Y), jnp.int32), vm((C, K, Y), f32),
            vm((S, 2, 128), jnp.int32), vm((S, 2, 2, 128), f32),
            vm((NZ, 128), f32), vm((KR, 128), f32), vm((KR, 128), f32),
            vm((16, 8, 128), f32), vm((16, 8, 128), f32),
            vm((2, 128), jnp.int32), vm((2, 2, 128), f32),
            vm((S, 8, Y), f32), vm((S, 8, Y), f32), vm((X, C, KR, Y), f32), vm((X + 2, C, KR, Y), f32),
            dma((2,)), dma, dma((2,)), dma((2,)),
            dma, dma((CHUNKS,)), dma, dma((CHUNKS + 1,)),
            dma((2,)), dma((2,)), dma((2,)), dma((2,)), dma((2,)), dma((2,)), dma, dma,
            dma((4,)), dma((4,)), dma((2,)), dma((2,)),
        ],
        compiler_params=pltpu.CompilerParams(
            collective_id=0, has_side_effects=True, vmem_limit_bytes=64_350_000
        ),
    )(
        forcing.reshape(C, Z, X, 1, Y),
        initial_state.reshape(K, C, 2, X, 1, Y),
        diagonal, span_speed, coupling.transpose(1, 0, 2), stiffener_mask, face_index, mode_shapes,
        jnp.asarray(high), jnp.asarray(low),
    )
    return flow.reshape(K, C, 2, X, Y), forces


def solution(mesh):
    return jax.shard_map(
        shards,
        mesh=mesh,
        in_specs=(
            P(None, "span", "stream", None),
            P("span", None, None, "stream", None),
            P(),
            P(),
            P(),
            P(),
            P(None, ("stream", "span")),
            P(None, None, ("stream", "span")),
        ),
        out_specs=(P("span", None, None, "stream", None), P()),
        check_vma=False,
    )
```
